128 devices in a mesh: layer: 8 (over y, core), lat: 16 (over x, z).
Axes of the slice: x: 4, y: 4, z: 4, core: 2. Of those that a mesh axis runs over, the one named last changes fastest.
Arguments:
- residuals: bfloat16 [8, 1024, 2048], P(None, ('layer', 'lat')), may hold values from -1100 to 1100
- topk_slots: int32 [8, 1024, 64], P(None, ('layer', 'lat')), may hold values from -1 to 65535, as said below
- dictionary: bfloat16 [8, 65536, 2048], P('layer', 'lat'), may hold values from -80 to 80
- enc_bias: float32 [8, 65536], P('layer', 'lat'), may hold values from 0.5 to 3
- dec_bias: float32 [8, 2048], P('layer'), may hold values from -5 to 5
- dead_ids: int32 [8, 256], P('layer'), may hold values from 0 to 65535, as said below
- seed_tokens: int32 [8, 256], P('layer'), may hold values from 0 to 1023
Outputs:
- reconstruction: bfloat16 [8, 1024, 2048], P(None, ('layer', 'lat'))
- unexplained: float32 [8], P('layer')
- latent_mass: float32 [8, 65536], P('layer', 'lat')
- new_rows: bfloat16 [8, 256, 2048], P('layer', 'lat')
- new_bias: float32 [8, 65536], P('layer', 'lat')
The draws below stay inside these ranges and needn't reach their ends.
Inputs may be any that keep to these rules, and one draw needn't show every extreme that they name: `topk_slots`: slot s of a token belongs to latent shard s // 4: it holds -1 or an id from (s // 4) * 4096 to (s // 4 + 1) * 4096 - 1. Every token has exactly 32 slots that are not -1; ids may repeat. In every layer some token fills all 4 slots of one shard. `dead_ids`: the 256 ids of one layer are distinct.
All inputs are finite; a program needn't handle non-finite values.
Results may differ from the reference program's by a relative error of at most 0.009.
Values may be sent and summed in bfloat16 or wider, within the bound.
A program may use at most 128 MiB of HBM per device.

```python
import math
import jax
import jax.numpy as jnp
from jax import lax

D = 2048
LAT_DEV = 4096
LATENTS = 65536
K = 32
SLOTS = 64
TOK_DEV = 8
LAYERS = 8
TOKENS = 1024
R = 256
N_LAT = 16


def draw_residuals(key, part):
    first, second, third = jax.random.split(key, 3)
    tok_index = jnp.arange(TOKENS)
    ramp = jnp.sqrt(1.0 + 2.0 * (tok_index // TOK_DEV % N_LAT).astype(jnp.float32) / max(N_LAT - 1, 1))
    rough = jnp.exp(jax.random.uniform(first, (LAYERS, TOKENS, 1), jnp.float32, 0.0, math.log(10.0)))
    column = jnp.exp(jax.random.uniform(second, (LAYERS, 1, D), jnp.float32, 0.0, math.log(10.0)))
    base = jnp.clip(jax.random.normal(third, (LAYERS, TOKENS, D), jnp.float32), -4.0, 4.0)
    return (base * rough * column * ramp[None, :, None]).astype(jnp.bfloat16)


def draw_topk_slots(key, part):
    first, second, third, fourth = jax.random.split(key, 4)
    row_count = LAYERS * TOKENS
    slot_cap = SLOTS // N_LAT
    row_keys = jax.random.split(first, row_count)
    ranks = jax.vmap(lambda subkey: jax.random.permutation(subkey, SLOTS))(row_keys).astype(jnp.int32)
    special_tok = jax.random.randint(second, (LAYERS,), 0, TOKENS)
    special_shard = jax.random.randint(third, (LAYERS,), 0, N_LAT)
    row_layer = jnp.arange(row_count) // TOKENS
    row_tok = jnp.arange(row_count) % TOKENS
    slot_shard = jnp.arange(SLOTS) // slot_cap
    boosted = (row_tok == special_tok[row_layer])[:, None] & (slot_shard[None, :] == special_shard[row_layer][:, None])
    score = ranks - SLOTS * boosted.astype(jnp.int32)
    order = jnp.argsort(jnp.argsort(score, axis=1, stable=True), axis=1, stable=True)
    is_live = order < K
    offsets = jax.random.randint(fourth, (row_count, SLOTS), 0, LAT_DEV)
    latent_ids = jnp.where(is_live, slot_shard[None, :] * LAT_DEV + offsets, -1)
    return latent_ids.reshape(LAYERS, TOKENS, SLOTS).astype(jnp.int32)


def draw_dictionary(key, part):
    first, second = jax.random.split(key, 2)
    lat_index = jnp.arange(LATENTS)
    ramp = jnp.sqrt(1.0 + 2.0 * (lat_index // LAT_DEV).astype(jnp.float32) / max(N_LAT - 1, 1))
    rough = jnp.exp(jax.random.uniform(first, (LAYERS, LATENTS, 1), jnp.float32, 0.0, math.log(10.0)))
    base = jnp.clip(jax.random.normal(second, (LAYERS, LATENTS, D), jnp.float32), -4.0, 4.0)
    return (base * rough * ramp[None, :, None]).astype(jnp.bfloat16)


def draw_dead_ids(key, part):
    layer_keys = jax.random.split(key, LAYERS)
    chosen = jax.vmap(lambda subkey: jax.random.permutation(subkey, LATENTS)[:R])(layer_keys)
    return chosen.astype(jnp.int32)


def with_ends(values, rng, least, high):
    longest = values.shape.index(max(values.shape))
    spots = []
    for shift in (0, 1):
        where = [jax.random.randint(jax.random.fold_in(rng, axis), (), 0, length) for axis, length in enumerate(values.shape)]
        where[longest] = (where[longest] + shift) % values.shape[longest]
        spots.append(tuple(where))
    return values.at[spots[0]].set(least).at[spots[1]].set(high)


def steps_of(rng, extent, cuts, low, largest):
    loudness = 1.0
    for dim, shards_of in cuts:
        heights = jax.random.uniform(jax.random.fold_in(jax.random.fold_in(rng, 6), dim), (shards_of,), jnp.float32, low / len(cuts), largest / len(cuts))
        loudness = loudness * jnp.repeat(jnp.exp(heights), extent[dim] // shards_of).reshape((-1,) + (1,) * (len(extent) - 1 - dim))
    return loudness


def centred(key, shape, width, reach, pieces=(), held_as=jnp.bfloat16):
    result = width * jax.random.normal(key, shape, jnp.float32)
    if pieces:
        result = result * steps_of(key, shape, pieces, -0.22, 0.18)
    return jnp.clip(result, -reach, reach).astype(held_as)


def setup_inputs(seed: int = 0) -> dict:
    splits = jax.random.split(jax.random.key(seed), 8)
    residuals = draw_residuals(jax.random.fold_in(splits[7], 71), 0)
    topk_slots = draw_topk_slots(jax.random.fold_in(splits[7], 71), 0)
    dictionary = draw_dictionary(jax.random.fold_in(splits[7], 71), 0)
    enc_bias = jnp.clip(0.5 + 2.5 * jax.random.uniform(splits[3], (LAYERS, LATENTS), jnp.float32) ** steps_of(splits[3], (LAYERS, LATENTS), ((0, 8), (1, 16)), -0.2, 0.2), 0.5, 3.0)
    dec_bias = centred(splits[4], (LAYERS, D), 1.0, 5.0, ((0, 8),), jnp.float32)
    dead_ids = draw_dead_ids(jax.random.fold_in(splits[7], 71), 0)
    seed_tokens = with_ends(jax.random.randint(splits[6], (LAYERS, R), 0, TOKENS), jax.random.fold_in(splits[6], 1), 0, TOKENS - 1).astype(jnp.int32)
    return dict(residuals=residuals, topk_slots=topk_slots, dictionary=dictionary, enc_bias=enc_bias, dec_bias=dec_bias, dead_ids=dead_ids, seed_tokens=seed_tokens)


def layer_terms(packed):
    normed, latent_ids, table, enc_row, dec_row, dead_row, seed_row = packed
    row_norms = jnp.sqrt(lax.optimization_barrier(jnp.sum(jnp.square(table.astype(jnp.float32)), axis=1)) + 1e-06)
    shifts = jnp.dot(table.astype(jnp.float32), dec_row, precision=lax.Precision.HIGHEST)
    is_live = latent_ids >= 0
    clipped = jnp.where(is_live, latent_ids, 0).astype(jnp.int32)

    def block_terms(block):
        feats, picks, live_block = block
        picked = jnp.take(table, picks, axis=0).astype(jnp.float32)
        products = jnp.einsum('td,tsd->ts', feats.astype(jnp.float32), picked, precision=lax.Precision.HIGHEST)
        preact = (products - shifts[picks]) / row_norms[picks] + enc_row[picks]
        activity = jnp.where(live_block, jnp.maximum(preact, 0.0), 0.0)
        rounded = lax.optimization_barrier((activity / row_norms[picks]).astype(jnp.bfloat16))
        coefficient = rounded.astype(jnp.float32)
        estimate = dec_row + jnp.einsum('ts,tsd->td', coefficient, picked, precision=lax.Precision.HIGHEST)
        return (estimate, activity)
    block_count = TOKENS // TOK_DEV
    estimate, activity = lax.map(block_terms, (normed.reshape(block_count, TOK_DEV, D), clipped.reshape(block_count, TOK_DEV, SLOTS), is_live.reshape(block_count, TOK_DEV, SLOTS)))
    estimate = estimate.reshape(TOKENS, D)
    activity = activity.reshape(TOKENS, SLOTS)
    feat32 = normed.astype(jnp.float32)
    errors = feat32 - estimate
    centered = feat32 - lax.optimization_barrier(jnp.mean(feat32, axis=0))
    unexplained = jnp.sum(jnp.square(errors)) / jnp.sum(jnp.square(centered))
    latent_mass = jax.ops.segment_sum(activity.reshape(-1), clipped.reshape(-1), num_segments=LATENTS)
    seeds = jnp.take(errors, seed_row, axis=0)
    seed_norm = jnp.sqrt(lax.optimization_barrier(jnp.sum(jnp.square(seeds), axis=1, keepdims=True)) + 1e-06)
    new_rows = (seeds / seed_norm * jnp.mean(row_norms)).astype(jnp.bfloat16)
    new_bias = enc_row.at[dead_row].set(0.0)
    return (estimate.astype(jnp.bfloat16), unexplained, latent_mass, new_rows, new_bias)

def reference(residuals, topk_slots, dictionary, enc_bias, dec_bias, dead_ids, seed_tokens):
    wide = residuals.astype(jnp.float32)
    mean_square = lax.optimization_barrier(jnp.mean(jnp.square(wide), axis=(1, 2)))
    normed = (wide * lax.rsqrt(mean_square)[:, None, None]).astype(jnp.bfloat16)
    reconstruction, unexplained, latent_mass, new_rows, new_bias = lax.map(layer_terms, (normed, topk_slots, dictionary, enc_bias, dec_bias, dead_ids, seed_tokens))
    return (reconstruction, unexplained, latent_mass, new_rows, new_bias)
```

```python
import functools

import jax
import jax.numpy as jnp
from jax import lax
from jax.experimental import pallas as pl
from jax.experimental.pallas import tpu as pltpu
from jax.sharding import Mesh
from jax.sharding import PartitionSpec as P

LAT = ("lat_0", "lat_1")
LAYER = ("layer_0", "layer_1")
LAYER_LAT = ("layer_0", "layer_1", "lat_0", "lat_1")
TILE = 512
BLOCK = 256


def split_up(shard, dim, size):
    before, after = (shard.shape[:dim], shard.shape[dim + 1 :])
    return jnp.moveaxis(shard.reshape(*before, size, -1, *after), dim, 0)


def joined_along(parts, dim):
    lengths = list(parts.shape[1:])
    lengths[dim] *= parts.shape[0]
    return jnp.moveaxis(parts, 0, dim).reshape(lengths)


def joined_exchange(shard, axis, axes, splits, concats):
    sizes = [lax.axis_size(a) for a in axes]
    parts = split_up(shard, splits[0], sizes[0])
    parts = jnp.moveaxis(split_up(parts, splits[1] + 1, sizes[1]), 0, 1)
    inside = parts.shape[2:]
    parts = parts.reshape(-1, *inside)
    parts = lax.all_to_all(parts, axis, split_axis=0, concat_axis=0, tiled=True)
    parts = joined_along(parts.reshape(*sizes, *inside), concats[0] + 1)
    return joined_along(parts, concats[1])


def token_position(global_tokens, tok_dev, lat_count, tok_group):
    blocks = global_tokens // tok_dev
    return blocks % lat_count * tok_group + blocks // lat_count * tok_dev + global_tokens % tok_dev


def row_stats(w, dec, shift, inv, norm, j):
    d = w.shape[1]
    sq = dc = None
    for g in range(d // 128):
        piece = w[pl.ds(j * TILE, TILE), g * 128 : (g + 1) * 128].astype(jnp.float32)
        a, b = piece * piece, piece * dec[0:1, g * 128 : (g + 1) * 128]
        sq, dc = (a, b) if sq is None else (sq + a, dc + b)
    ones = jnp.ones((8, 128), jnp.float32)
    dims = (((1,), (1,)), ((), ()))
    hi = lax.Precision.HIGHEST
    total = lax.dot_general(ones, sq, dims, precision=hi, preferred_element_type=jnp.float32)
    n = jnp.sqrt(total + 1e-06)
    norm[j] = n
    inv[j] = 1.0 / n
    shift[j] = lax.dot_general(ones, dc, dims, precision=hi, preferred_element_type=jnp.float32)


def encode_tile(feats, w, slot, shift, inv, enc, mass, coef, j):
    wt = w[pl.ds(j * TILE, TILE), :]
    p = lax.dot_general(feats[...], wt, (((1,), (1,)), ((), ())), preferred_element_type=jnp.float32)
    rows = p.shape[0]
    p = p.reshape(rows // 8, 8, TILE)
    act = jnp.maximum((p - shift[j]) * inv[j] + enc[j], 0.0)
    kept = []
    for g in range(TILE // 128):
        a = act[:, :, g * 128 : (g + 1) * 128]
        base = (j * TILE + g * 128).astype(jnp.float32)
        total = None
        for c in range(4):
            hit = jnp.where(slot[c] == base, a, 0.0)
            total = hit if total is None else total + hit
        kept.append(total)
    kept = jnp.concatenate(kept, axis=2)
    mass[j] += jnp.sum(kept, axis=0)
    at = pl.ds(pl.multiple_of(j * TILE, TILE), TILE)
    coef[:, at] = (kept * inv[j]).reshape(rows, TILE).astype(jnp.bfloat16)


def dense_kernel(feats, w, dec, enc, slots, part, mass, norm, shift, inv, slot, coef):
    tiles = w.shape[0] // TILE

    @pl.when(pl.program_id(0) == 0)
    def _():
        mass[...] = jnp.zeros_like(mass)
        lax.fori_loop(0, tiles, lambda j, _: row_stats(w, dec, shift, inv, norm, j), None)

    lanes = lax.broadcasted_iota(jnp.int32, (BLOCK, 128), 1)
    for c in range(4):
        delta = slots[:, c : c + 1] - lanes
        slot[c] = delta.astype(jnp.float32).reshape(BLOCK // 8, 8, 128)

    lax.fori_loop(
        0, tiles, lambda j, _: encode_tile(feats, w, slot, shift, inv, enc, mass, coef, j), None
    )

    @pl.loop(0, w.shape[1] // TILE)
    def _(n):
        at = pl.ds(pl.multiple_of(n * TILE, TILE), TILE)
        part[:, at] = jnp.dot(coef[...], w[:, at], preferred_element_type=jnp.float32).astype(jnp.bfloat16)


def dense(features, rows, dec, enc, slots):
    tokens, d = features.shape
    lats = rows.shape[0]
    tiles = lats // TILE
    whole = lambda *shape: pl.BlockSpec(
        shape, lambda b: (0,) * len(shape), pipeline_mode=pl.Buffered(1)
    )
    stat = (tiles, 8, TILE)
    enc8 = jnp.broadcast_to(enc.reshape(tiles, 1, TILE), stat)
    return pl.pallas_call(
        dense_kernel,
        out_shape=(
            jax.ShapeDtypeStruct((tokens, d), jnp.bfloat16),
            jax.ShapeDtypeStruct(stat, jnp.float32),
            jax.ShapeDtypeStruct(stat, jnp.float32),
        ),
        grid=(tokens // BLOCK,),
        in_specs=[
            pl.BlockSpec((BLOCK, d), lambda b: (b, 0)),
            whole(lats, d),
            whole(1, d),
            whole(*stat),
            pl.BlockSpec((BLOCK, 4), lambda b: (b, 0)),
        ],
        out_specs=(pl.BlockSpec((BLOCK, d), lambda b: (b, 0)), whole(*stat), whole(*stat)),
        scratch_shapes=[
            pltpu.VMEM(stat, jnp.float32),
            pltpu.VMEM(stat, jnp.float32),
            pltpu.VMEM((4, BLOCK // 8, 8, 128), jnp.float32),
            pltpu.VMEM((BLOCK, lats), jnp.bfloat16),
        ],
        compiler_params=pltpu.CompilerParams(vmem_limit_bytes=56 * 2**20),
        name="dense",
    )(features, rows, dec, enc8, slots)


def body(residuals, topk_slots, dictionary, enc_bias, dec_bias, dead_ids, seed_tokens):
    tok_dev = residuals.shape[1]
    lat_count = lax.axis_size(LAT)
    layer_size = lax.axis_size(LAYER)
    shard_index = lax.axis_index(LAT)
    lat_dev = dictionary.shape[1]
    tok_group = tok_dev * layer_size
    regrouped = lax.all_to_all(residuals, LAYER, split_axis=0, concat_axis=1, tiled=True)
    gathered = lax.all_gather(regrouped, LAT, axis=1, tiled=True)[0]
    mine_slots = joined_exchange(topk_slots, LAYER_LAT, (LAYER, LAT), (0, 2), (1, 1))[0]
    wide = gathered.astype(jnp.float32)
    scale = lax.rsqrt(jnp.mean(jnp.square(wide)))
    features = (wide * scale).astype(jnp.bfloat16)
    local_slots = jnp.where(mine_slots >= 0, mine_slots - shard_index * lat_dev, -(2**16))
    partial_value, mass8, norm8 = dense(
        features, dictionary[0], dec_bias, enc_bias[0], local_slots
    )
    latent_mass = jnp.sum(mass8, axis=1).reshape(1, lat_dev)
    norm_sum = lax.psum(jnp.sum(norm8[:, 0, :]), LAT)
    r_dev = seed_tokens.shape[1] // lat_count
    summed = lax.psum(partial_value, LAT).astype(jnp.float32)
    estimate = summed + dec_bias[0]
    errors = features.astype(jnp.float32) - estimate
    numerator = jnp.sum(jnp.square(errors))
    estimate_own = lax.dynamic_slice_in_dim(estimate, shard_index * tok_group, tok_group, 0)
    my_seeds = lax.dynamic_slice_in_dim(seed_tokens[0], shard_index * r_dev, r_dev, 0)
    seeds = jnp.take(errors, token_position(my_seeds, tok_dev, lat_count, tok_group), axis=0)
    feat32 = features.astype(jnp.float32)
    centered = feat32 - jnp.mean(feat32, axis=0)
    denominator = jnp.sum(jnp.square(centered))
    unexplained = (numerator / denominator).reshape(1)
    seed_norm = jnp.sqrt(jnp.sum(jnp.square(seeds), axis=1, keepdims=True) + 1e-06)
    new_rows = (seeds / seed_norm * (norm_sum / (lat_dev * lat_count))).astype(jnp.bfloat16)[None]
    candidates = shard_index * lat_dev + jnp.arange(lat_dev, dtype=jnp.int32)
    is_dead = jnp.any(dead_ids[0][:, None] == candidates[None, :], axis=0)
    new_bias = jnp.where(is_dead, 0.0, enc_bias[0])[None]
    reconstruction = lax.all_to_all(
        estimate_own.astype(jnp.bfloat16)[None], LAYER, split_axis=1, concat_axis=0, tiled=True
    )
    return (reconstruction, unexplained, latent_mass, new_rows, new_bias)


def solution(mesh):
    split = Mesh(mesh.devices.reshape(4, 2, 4, 4), ("layer_0", "layer_1", "lat_0", "lat_1"))
    placed = (
        P(None, LAYER_LAT, None),
        P(None, LAYER_LAT, None),
        P(LAYER, LAT, None),
        P(LAYER, LAT),
        P(LAYER, None),
        P(LAYER, None),
        P(LAYER, None),
    )
    return jax.shard_map(
        body,
        mesh=split,
        in_specs=placed,
        out_specs=(
            P(None, LAYER_LAT, None),
            P(LAYER),
            P(LAYER, LAT),
            P(LAYER, LAT, None),
            P(LAYER, LAT),
        ),
        check_vma=False,
    )
```

```python
import jax
import jax.numpy as jnp
from jax import lax
from jax.experimental import pallas as pl
from jax.experimental.pallas import tpu as pltpu
from jax.sharding import Mesh
from jax.sharding import PartitionSpec as P

Y, C, X, Z = "layer_0", "layer_1", "lat_0", "lat_1"
LAT = (X, Z)
LAYER = (Y, C)
LAYER_LAT = (Y, C, X, Z)
MESH = pl.DeviceIdType.MESH
NT = (((1,), (1,)), ((), ()))
F32 = jnp.float32
BF16 = jnp.bfloat16
TILE = 1024
STAT = 512
COLS = 1024
TOK = 8
HALF = 32
BLOCK = 256
RES = 8

TO_LAYER, FIRST, NEAR, RELAY, SQUARE, SHARE, SEEDS, LAST, LAST_SEEDS, FINAL, BACK, COUNT = (
    0, 8, 14, 18, 22, 38, 44, 50, 56, 62, 78, 86
)


def row_stats(w, dec, shift, inv, norm, j):
    sq = dc = None
    for g in range(w.shape[1] // 128):
        at = slice(g * 128, (g + 1) * 128)
        piece = w[pl.ds(j * STAT, STAT), at].astype(F32)
        a, b = piece * piece, piece * dec[0:1, at]
        sq, dc = (a, b) if sq is None else (sq + a, dc + b)
    ones = jnp.ones((8, 128), F32)
    hi = lax.Precision.HIGHEST
    total = lax.dot_general(ones, sq, NT, precision=hi, preferred_element_type=F32)
    n = jnp.sqrt(total + 1e-06)
    norm[j] = n
    inv[j] = 1.0 / n
    shift[j] = lax.dot_general(ones, dc, NT, precision=hi, preferred_element_type=F32)


def encode_tile(feats, w, slot, shift, inv, enc, mass, coef, p, j):
    p[...] = lax.dot_general(
        feats[...], w[pl.ds(j * TILE, TILE), :], NT, preferred_element_type=F32
    )
    for g in range(TILE // 128):
        s = j * (TILE // STAT) + g // (STAT // 128)
        at = slice(g % (STAT // 128) * 128, (g % (STAT // 128) + 1) * 128)
        iv = inv[s, :, at]
        pre = p[:, g * 128 : (g + 1) * 128].reshape(BLOCK // 8, 8, 128)
        act = jnp.maximum((pre - shift[s, :, at]) * iv + enc[s, :, at], 0.0)
        base = (j * TILE + g * 128).astype(F32)
        total = None
        for c in range(4):
            hit = jnp.where(slot[c] == base, act, 0.0)
            total = hit if total is None else total + hit
        mass[s, :, at] += jnp.sum(total, axis=0)
        to = pl.ds(pl.multiple_of(j * TILE + g * 128, 128), 128)
        coef[:, to] = (total * iv).reshape(BLOCK, 128).astype(BF16)


def kernel(
    aug, w_hbm, dec, enc, pos, recon, unexplained, mass, new_rows,
    w, own, fa, fb, nf, slot, coef, p, part, ra, rb, seeds, rsa, rsb,
    sa, sb, ta, tb, ssa, ssb, tsa, tsb, squares, finals, shift, inv, norm, rec,
    send, recv, wsem, osem,
):
    d = w.shape[1]
    lats = w.shape[0]
    y, c, x, z = (lax.axis_index(a) for a in (Y, C, X, Z))
    me = 2 * y + c
    tokens = 4 * BLOCK

    def ring(at, step):
        return lax.rem(at + step, 4)

    def push(src, dst, n, device):
        copy = pltpu.make_async_remote_copy(
            src_ref=src, dst_ref=dst, send_sem=send.at[n], recv_sem=recv.at[n],
            device_id=device, device_id_type=MESH,
        )
        return copy

    def local(src, dst, n):
        return pltpu.make_async_copy(src, dst, osem.at[n])

    sent = []

    def start(copies):
        for copy in copies:
            copy.start()
        sent.extend(copies)

    def arrive(copies):
        for copy in copies:
            copy.wait_recv()

    rows = lats // 4
    loads = [
        pltpu.make_async_copy(w_hbm.at[pl.ds(q * rows, rows)], w.at[pl.ds(q * rows, rows)], wsem.at[q])
        for q in range(4)
    ]
    for load in loads:
        load.start()

    column = [(dy, dc) for dy in range(4) for dc in range(2) if dy or dc]
    plane = [(dx, dz) for dx in range(4) for dz in range(4) if dx or dz]

    def in_column(dy, dc):
        return {Y: ring(y, dy), C: lax.rem(c + dc, 2)}

    def in_plane(dx, dz):
        return {X: ring(x, dx), Z: ring(z, dz)}

    barrier = pltpu.get_barrier_semaphore()
    for dy, dc in column:
        pl.semaphore_signal(barrier, inc=1, device_id=in_column(dy, dc), device_id_type=MESH)
    for dx, dz in plane:
        pl.semaphore_signal(barrier, inc=1, device_id=in_plane(dx, dz), device_id_type=MESH)
    pl.semaphore_wait(barrier, len(column) + len(plane))

    to_layer = []
    for dy, dc in column:
        g = 2 * ring(y, dy) + lax.rem(c + dc, 2)
        to_layer.append(push(aug.at[g], own.at[me], TO_LAYER + 2 * dy + dc, in_column(dy, dc)))
    start(to_layer)
    mine = local(aug.at[me], own.at[me], 0)
    mine.start()

    def stats(q):
        loads[q].wait()
        per = rows // STAT
        lax.fori_loop(
            q * per, (q + 1) * per, lambda j, _: row_stats(w, dec, shift, inv, norm, j), None
        )

    stats(0)
    mass[...] = jnp.zeros_like(mass)
    mine.wait()
    arrive(to_layer)

    half = TOK // 2
    first = []
    for k in (1, 3, 2):
        first.append(push(own.at[pl.ds(0, half)], fa.at[z, x], FIRST + k - 1, {X: ring(x, k)}))
        first.append(push(own.at[pl.ds(half, half)], fb.at[x, z], FIRST + 2 + k, {Z: ring(z, k)}))
    start(first)
    keep = [local(own.at[pl.ds(0, half)], fa.at[z, x], 1), local(own.at[pl.ds(half, half)], fb.at[x, z], 2)]
    for copy in keep:
        copy.start()

    def add_squares(g, acc):
        v = own[g, :, pl.ds(0, d)].astype(F32)
        return acc + v * v

    square = jnp.sum(lax.fori_loop(0, TOK, add_squares, jnp.zeros((TOK, d), F32)))
    here = 4 * x + z
    squares[here] = jnp.full((8, 128), square, F32)
    square_copies = [
        push(squares.at[here], squares.at[here], SQUARE + 4 * dx + dz, in_plane(dx, dz))
        for dx, dz in plane
    ]
    start(square_copies)
    stats(1)
    for copy in keep:
        copy.wait()
    arrive(first)
    near = []
    for e, k in enumerate((1, 3)):
        near.append(push(fa.at[z], fa.at[z], NEAR + 2 * e, {Z: ring(z, k)}))
        near.append(push(fb.at[x], fb.at[x], NEAR + 2 * e + 1, {X: ring(x, k)}))
    start(near)
    stats(2)
    stats(3)
    arrive(square_copies)
    scale = lax.rsqrt(jnp.sum(squares[...], axis=0)[0:1, 0:1] / (tokens * d))

    pick_row = lax.broadcasted_iota(jnp.int32, (128, 512), 0)
    pick_slot = lax.broadcasted_iota(jnp.int32, (128, 512), 1) // 128 + 4 * here
    pick = jnp.where(pick_row == pick_slot, 64.0, 0.0) + jnp.where(pick_row == pick_slot + 64, 1.0, 0.0)
    pick = pick.astype(BF16)

    up, down = pl.ds(0, 2), pl.ds(2, 2)
    relay = [
        push(fa.at[ring(z, 3), up], fa.at[ring(z, 3), up], RELAY, {Z: ring(z, 1)}),
        push(fa.at[ring(z, 1), down], fa.at[ring(z, 1), down], RELAY + 1, {Z: ring(z, 3)}),
        push(fb.at[ring(x, 3), up], fb.at[ring(x, 3), up], RELAY + 2, {X: ring(x, 1)}),
        push(fb.at[ring(x, 1), down], fb.at[ring(x, 1), down], RELAY + 3, {X: ring(x, 3)}),
    ]
    sent.extend(relay)

    def share(k):
        return [
            push(part.at[k, pl.ds(0, 128)], ra.at[k - 1], SHARE + k - 1, {Z: ring(z, k)}),
            push(part.at[k, pl.ds(128, 128)], rb.at[k - 1], SHARE + 2 + k, {X: ring(x, k)}),
        ]

    def block(step, _):
        k = step + step // 2 - 2 * (step // 3)

        @pl.when(step == 1)
        def _():
            arrive(near)
            for copy in relay:
                copy.start()

        @pl.when(step == 3)
        def _():
            arrive(relay)

        lane = lax.broadcasted_iota(jnp.int32, (16, 8, 128), 2).astype(F32)
        for h, buf, at in ((0, fa, ring(z, k)), (1, fb, ring(x, k))):

            def normalize(q, _, h=h, buf=buf, at=at):
                v = buf[at, q, :, :, pl.ds(0, d)].astype(F32).reshape(HALF, d) * scale
                nf[k, pl.ds(h * 128 + q * HALF, HALF), :] = v.astype(BF16)

            lax.fori_loop(0, 4, normalize, None)
            tail = buf[at, :, :, :, pl.ds(d, 128)].astype(F32).reshape(128, 128).astype(BF16)
            ids = jnp.dot(tail, pick, preferred_element_type=F32)
            for s in range(4):
                slot[s, pl.ds(16 * h, 16)] = ids[:, s * 128 : (s + 1) * 128].reshape(16, 8, 128) - lane

        lax.fori_loop(
            0,
            lats // TILE,
            lambda j, _: encode_tile(nf.at[k], w, slot, shift, inv, enc, mass, coef, p, j),
            None,
        )

        @pl.loop(0, d // COLS)
        def _(n):
            at = pl.ds(pl.multiple_of(n * COLS, COLS), COLS)
            part[k, :, at] = jnp.dot(coef[...], w[:, at], preferred_element_type=F32).astype(BF16)

        @pl.when(step > 0)
        def _():
            for copy in share(k):
                copy.start()

    lax.fori_loop(0, 4, block, None)
    shares = share(1) + share(3) + share(2)
    sent.extend(shares)

    spots = lax.broadcasted_iota(jnp.int32, (4 * 2 * 4 * RES, 128), 1)
    onehot = jnp.concatenate(
        [jnp.where(pos[...] - q * 128 == spots, 1.0, 0.0) for q in range(tokens // 128)], axis=1
    ).astype(BF16)

    @pl.loop(0, d // 512)
    def _(n):
        at = pl.ds(pl.multiple_of(n * 512, 512), 512)
        v = jnp.dot(onehot, part[:, :, at].reshape(tokens, 512), preferred_element_type=F32)
        seeds[:, :, :, :, at] = v.reshape(4, 2, 4, RES, 512).astype(BF16)

    seed_copies = []
    for k in (2, 1, 3):
        seed_copies.append(push(seeds.at[k, 0], rsa.at[k - 1], SEEDS + k - 1, {Z: ring(z, k)}))
        seed_copies.append(push(seeds.at[k, 1], rsb.at[k - 1], SEEDS + 2 + k, {X: ring(x, k)}))
    start(seed_copies)
    arrive(shares)

    def add_shares(q, _):
        at = pl.ds(q * HALF, HALF)
        for to, got, lo in ((sa, ra, 0), (sb, rb, 128)):
            v = part[0, pl.ds(lo + q * HALF, HALF), :].astype(F32)
            for k in range(3):
                v = v + got[k, at, :].astype(F32)
            to[q] = v.astype(BF16)

    lax.fori_loop(0, 4, add_shares, None)
    last = []
    for k in (1, 3, 2):
        last.append(push(sa.at[ring(x, k)], ta.at[k - 1], LAST + k - 1, {X: ring(x, k)}))
        last.append(push(sb.at[ring(z, k)], tb.at[k - 1], LAST + 2 + k, {Z: ring(z, k)}))
    start(last)
    arrive(seed_copies)

    def add_seeds(q, _):
        for to, got, h in ((ssa, rsa, 0), (ssb, rsb, 1)):
            v = seeds[0, h, q].astype(F32)
            for k in range(3):
                v = v + got[k, q].astype(F32)
            to[q] = v.astype(BF16)

    lax.fori_loop(0, 4, add_seeds, None)
    last_seeds = []
    for k in (1, 3, 2):
        last_seeds.append(push(ssa.at[ring(x, k)], tsa.at[k - 1], LAST_SEEDS + k - 1, {X: ring(x, k)}))
        last_seeds.append(push(ssb.at[ring(z, k)], tsb.at[k - 1], LAST_SEEDS + 2 + k, {Z: ring(z, k)}))
    start(last_seeds)

    def add_tokens(q, acc):
        for k in range(4):
            acc = acc + nf[k, pl.ds(q * 16, 16), :].astype(F32)
        return acc

    sums = lax.fori_loop(0, BLOCK // 16, add_tokens, jnp.zeros((16, d), F32))
    means = jnp.sum(sums, axis=0, keepdims=True) / tokens
    my_pos = jnp.concatenate([pos[pl.ds(x * RES, RES), :], pos[pl.ds(4 * RES + z * RES, RES), :]], axis=0)
    my_spots = lax.broadcasted_iota(jnp.int32, (2 * RES, 128), 1)
    my_onehot = jnp.concatenate(
        [jnp.where(my_pos - q * 128 == my_spots, 1.0, 0.0) for q in range(tokens // 128)], axis=1
    ).astype(BF16)
    seed_feats = jnp.dot(my_onehot, nf[...].reshape(tokens, d), preferred_element_type=F32)
    norm_sum = jnp.sum(norm[...]) / 8.0

    arrive(last)
    numerator = denominator = None
    for h, mine_sum, got, lo in ((0, sa.at[x], ta, x * HALF), (1, sb.at[z], tb, 128 + z * HALF)):
        v = mine_sum[...].astype(F32)
        for k in range(3):
            v = v + got[k].astype(F32)
        v = v + dec[...]
        rec[pl.ds(h * half, half)] = v.reshape(half, TOK, d).astype(BF16)
        feats = nf[0, pl.ds(lo, HALF), :].astype(F32)
        e, m = feats - v, feats - means
        n_h, d_h = jnp.sum(e * e), jnp.sum(m * m)
        numerator = n_h if h == 0 else numerator + n_h
        denominator = d_h if h == 0 else denominator + d_h

    back = []
    for dy, dc in column:
        g = 2 * ring(y, dy) + lax.rem(c + dc, 2)
        back.append(push(rec.at[g], recon.at[me], BACK + 2 * dy + dc, in_column(dy, dc)))
    start(back)
    mine_back = local(rec.at[me], recon.at[me], 0)
    mine_back.start()
    which = lax.broadcasted_iota(jnp.int32, (8, 128), 0)
    finals[here] = jnp.where(which == 0, numerator, jnp.where(which == 1, denominator, norm_sum))
    final_copies = [
        push(finals.at[here], finals.at[here], FINAL + 4 * dx + dz, in_plane(dx, dz)) for dx, dz in plane
    ]
    start(final_copies)

    arrive(last_seeds)
    estimates = []
    for mine_sum, got in ((ssa.at[x], tsa), (ssb.at[z], tsb)):
        v = mine_sum[...].astype(F32)
        for k in range(3):
            v = v + got[k].astype(F32)
        estimates.append(v + dec[...])
    errors = seed_feats - jnp.concatenate(estimates, axis=0)
    seed_norm = jnp.sqrt(jnp.sum(errors * errors, axis=1, keepdims=True) + 1e-06)
    unit = errors / seed_norm
    arrive(final_copies)
    total = jnp.sum(finals[...], axis=0)
    unexplained[...] = jnp.broadcast_to(total[0:1, :] / total[1:2, :], (8, 128))
    new_rows[...] = (unit * (total[2:3, 0:1] / (lats * 16))).astype(BF16)
    mine_back.wait()
    arrive(back)
    for copy in sent:
        copy.wait_send()


def fused(aug, rows, dec, enc, pos):
    lats, d = rows.shape
    wide = aug.shape[2]
    stat = (lats // STAT, 8, STAT)
    enc8 = jnp.broadcast_to(enc.reshape(lats // STAT, 1, STAT), stat)
    vmem = pl.BlockSpec(memory_space=pltpu.VMEM)
    hbm = pl.BlockSpec(memory_space=pl.ANY)
    half = TOK // 2
    scratch = [
        ((lats, d), BF16),
        ((TOK, TOK, wide), BF16),
        ((4, 4, half, TOK, wide), BF16),
        ((4, 4, half, TOK, wide), BF16),
        ((4, BLOCK, d), BF16),
        ((4, BLOCK // 8, 8, 128), F32),
        ((BLOCK, lats), BF16),
        ((BLOCK, TILE), F32),
        ((4, BLOCK, d), BF16),
        ((3, 128, d), BF16),
        ((3, 128, d), BF16),
        ((4, 2, 4, RES, d), BF16),
        ((3, 4, RES, d), BF16),
        ((3, 4, RES, d), BF16),
        ((4, HALF, d), BF16),
        ((4, HALF, d), BF16),
        ((3, HALF, d), BF16),
        ((3, HALF, d), BF16),
        ((4, RES, d), BF16),
        ((4, RES, d), BF16),
        ((3, RES, d), BF16),
        ((3, RES, d), BF16),
        ((16, 8, 128), F32),
        ((16, 8, 128), F32),
        (stat, F32),
        (stat, F32),
        (stat, F32),
        ((TOK, TOK, d), BF16),
    ]
    return pl.pallas_call(
        kernel,
        out_shape=(
            jax.ShapeDtypeStruct((TOK, TOK, d), BF16),
            jax.ShapeDtypeStruct((8, 128), F32),
            jax.ShapeDtypeStruct(stat, F32),
            jax.ShapeDtypeStruct((2 * RES, d), BF16),
        ),
        in_specs=[hbm, hbm, vmem, vmem, vmem],
        out_specs=(vmem, vmem, vmem, vmem),
        scratch_shapes=[pltpu.VMEM(*s) for s in scratch]
        + [
            pltpu.SemaphoreType.DMA((COUNT,)),
            pltpu.SemaphoreType.DMA((COUNT,)),
            pltpu.SemaphoreType.DMA((4,)),
            pltpu.SemaphoreType.DMA((3,)),
        ],
        compiler_params=pltpu.CompilerParams(
            collective_id=0, has_side_effects=True, vmem_limit_bytes=60 * 2**20
        ),
        name="sae",
    )(aug, rows, dec, enc8, pos)


def seed_positions(seed_tokens, x, z):
    s = seed_tokens.reshape(4, 4, 2, RES)
    roll = lambda v, by: lax.dynamic_slice_in_dim(jnp.concatenate([v, v], 0), by, 4, 0)
    along_z = roll(s[:, :, 0].transpose(1, 0, 2), z)
    along_x = roll(s[:, :, 1], x)
    n = jnp.stack([along_z, along_x], 1).reshape(-1)
    home = n // TOK % 16
    xi, zi, g, t = home // 4, home % 4, n // (16 * TOK), n % TOK
    a = (zi - z) % 4 * BLOCK + xi * HALF + g * TOK + t
    b = (xi - x) % 4 * BLOCK + 128 + zi * HALF + (g - TOK // 2) * TOK + t
    pos = jnp.where(g < TOK // 2, a, b)
    return jnp.broadcast_to(pos[:, None], (pos.shape[0], 128))


def body(residuals, topk_slots, dictionary, enc_bias, dec_bias, dead_ids, seed_tokens):
    lat_dev = dictionary.shape[1]
    x, z = lax.axis_index(X), lax.axis_index(Z)
    shard = jnp.arange(topk_slots.shape[2], dtype=jnp.int32) // 4
    place = jnp.where(topk_slots >= 0, topk_slots - shard * lat_dev, lat_dev)
    aug = jnp.concatenate(
        [residuals, (place // 64).astype(BF16), (place % 64).astype(BF16)], axis=2
    )
    pos = seed_positions(seed_tokens[0], x, z)
    recon, unexplained, mass, new_rows = fused(aug, dictionary[0], dec_bias, enc_bias[0], pos)
    latent_mass = jnp.sum(mass, axis=1).reshape(1, lat_dev)
    candidates = (4 * x + z) * lat_dev + jnp.arange(lat_dev, dtype=jnp.int32)
    is_dead = jnp.any(dead_ids[0][:, None] == candidates[None, :], axis=0)
    new_bias = jnp.where(is_dead, 0.0, enc_bias[0])[None]
    return (recon, unexplained[0, 0:1], latent_mass, new_rows[None], new_bias)


def solution(mesh):
    split = Mesh(mesh.devices.reshape(4, 2, 4, 4), (Y, C, X, Z))
    placed = (
        P(None, LAYER_LAT, None),
        P(None, LAYER_LAT, None),
        P(LAYER, LAT, None),
        P(LAYER, LAT),
        P(LAYER, None),
        P(LAYER, None),
        P(LAYER, None),
    )
    return jax.shard_map(
        body,
        mesh=split,
        in_specs=placed,
        out_specs=(
            P(None, LAYER_LAT, None),
            P(LAYER),
            P(LAYER, LAT),
            P(LAYER, LAT, None),
            P(LAYER, LAT),
        ),
        check_vma=False,
    )
```

```python
import jax
import jax.numpy as jnp
from jax import lax
from jax.experimental import pallas as pl
from jax.experimental.pallas import tpu as pltpu
from jax.sharding import Mesh
from jax.sharding import PartitionSpec as P

Y, C, X, Z = "layer_0", "layer_1", "lat_0", "lat_1"
LAT = (X, Z)
LAYER = (Y, C)
LAYER_LAT = (Y, C, X, Z)
MESH = pl.DeviceIdType.MESH
NT = (((1,), (1,)), ((), ()))
F32 = jnp.float32
BF16 = jnp.bfloat16
TILE = 1024
STAT = 512
COLS = 1024
TOK = 8
HALF = 32
BLOCK = 256
RES = 8
GROUPS = TILE // 128

TO_LAYER, FIRST, AROUND, SQUARE, FAR, NEAR, SEEDS, LAST, LAST_SEEDS, FINAL, BACK, COUNT = (
    0, 8, 14, 24, 40, 42, 50, 56, 68, 74, 90, 98
)


def row_stats(w, decs, enc, inv, bias, norm, j):
    sq = None
    tile = pl.ds(j * STAT, STAT)
    for g in range(w.shape[1] // 128):
        piece = w[tile, g * 128 : (g + 1) * 128].astype(F32)
        a = piece * piece
        sq = a if sq is None else sq + a
    ones = jnp.ones((8, 128), F32)
    total = lax.dot_general(
        ones, sq, NT, precision=lax.Precision.HIGHEST, preferred_element_type=F32
    )
    parts = lax.dot_general(decs[...], w[tile, :], NT, preferred_element_type=F32)
    shift = jnp.sum(parts, axis=0, keepdims=True)
    n = jnp.sqrt(total + 1e-06)
    norm[...] += n
    iv = 1.0 / n
    for g in range(STAT // 128):
        at = slice(g * 128, (g + 1) * 128)
        row = j * (STAT // 128) + g
        inv[row] = iv[:, at]
        bias[row] = enc[pl.ds(row, 1), :] - shift[:, at] * iv[:, at]


def encode(feats, w, bits, inv, bias, mass, coef, p, between):
    tiles = w.shape[0] // TILE

    def product(j):
        p[j % 2] = lax.dot_general(
            feats[...], w[pl.ds(j * TILE, TILE), :], NT, preferred_element_type=F32
        )

    def activity(j):
        for g in range(GROUPS):
            row = j * GROUPS + g
            iv = inv[row]
            pre = p[j % 2, :, g * 128 : (g + 1) * 128].reshape(BLOCK // 8, 8, 128)
            count = ((bits[j] >> (4 * g)) & 15).astype(F32)
            total = jnp.maximum(pre * iv + bias[row], 0.0) * count
            mass[row] += jnp.sum(total, axis=0)
            coef[:, row * 128 : (row + 1) * 128] = (total * iv).reshape(BLOCK, 128).astype(BF16)

    product(0)
    for j in range(1, tiles):
        product(j)
        activity(j - 1)
        if j == 1:
            between()
    activity(tiles - 1)


def iota(shape, dim):
    return lax.broadcasted_iota(jnp.int32, shape, dim)


def seed_places(seeds, x, z):
    n = seeds[...]
    home, g, t = (n >> 3) & 15, n >> 7, n & 7
    xi, zi = home >> 2, home & 3
    is_a = g < 4
    far = jnp.where(is_a, zi - z, xi - x) & 3
    index = jnp.where(is_a, xi, zi)
    odd = (far & 1) == 1
    step = jnp.where(odd, 1 + ((g & 3) >> 1 << 1), far)
    inside = jnp.where(
        odd, (far >> 1) * 64 + index * 16 + (g & 1) * TOK, index * HALF + (g & 3) * TOK
    )
    place = step * BLOCK + jnp.where(is_a, 0, 128) + inside + t
    size = seeds.shape[1]
    row, col = iota((size, size), 0), iota((size, size), 1)
    k, h, i = row >> 6, (row >> 5) & 1, (row >> 3) & 3
    xr = jnp.where(h == 0, i, (x + k) & 3)
    zr = jnp.where(h == 0, (z + k) & 3, i)
    match = col == (xr * 4 + zr) * 16 + h * RES + (row & 7)
    ones = jnp.ones((size, 128), BF16)

    def column(v):
        kept = jnp.where(match, v.astype(F32), 0.0).astype(BF16)
        return jnp.dot(kept, ones, preferred_element_type=F32)

    return column(place >> 5) * 32.0 + column(place & 31)


def one_hot(places, count):
    spots = iota(places.shape, 1).astype(F32)
    return jnp.concatenate(
        [jnp.where(places - q * 128.0 == spots, 1.0, 0.0) for q in range(count // 128)], axis=1
    ).astype(BF16)


def kernel(
    res, slots, w_hbm, dec, enc, dead, seed_tokens,
    recon, unexplained, mass_out, new_rows, new_bias,
    w, aug, own, fa, fb, nf, bits, coef, p, part, fara, farb, near_in, picked, seeds, rsa, rsb,
    sa, sb, ta, tb, ssa, ssb, tsa, tsb, squares, finals, inv, bias, norm, mass, decs, places, rec,
    send, recv, wsem, osem,
):
    d = w.shape[1]
    lats = w.shape[0]
    y, c, x, z = (lax.axis_index(a) for a in (Y, C, X, Z))
    me = 2 * y + c
    here = 4 * x + z
    tokens = 4 * BLOCK

    def ring(at, step):
        return lax.rem(at + step, 4)

    def push(src, dst, n, device):
        return pltpu.make_async_remote_copy(
            src_ref=src, dst_ref=dst, send_sem=send.at[n], recv_sem=recv.at[n],
            device_id=device, device_id_type=MESH,
        )

    def local(src, dst, n):
        return pltpu.make_async_copy(src, dst, osem.at[n])

    sent = []

    def start(copies):
        for copy in copies:
            copy.start()
        sent.extend(copies)

    def arrive(copies):
        for copy in copies:
            copy.wait_recv()

    column = [(dy, dc) for dy in range(4) for dc in range(2) if dy or dc]
    plane = [(dx, dz) for dx in range(4) for dz in range(4) if dx or dz]

    def in_column(dy, dc):
        return {Y: ring(y, dy), C: lax.rem(c + dc, 2)}

    def in_plane(dx, dz):
        return {X: ring(x, dx), Z: ring(z, dz)}

    barrier = pltpu.get_barrier_semaphore()
    for dy, dc in column:
        pl.semaphore_signal(barrier, inc=1, device_id=in_column(dy, dc), device_id_type=MESH)
    for dx, dz in plane:
        pl.semaphore_signal(barrier, inc=1, device_id=in_plane(dx, dz), device_id_type=MESH)

    fill = local(res, aug.at[:, :, pl.ds(0, d)], 0)
    fill.start()
    rows = lats // 4
    loads = [
        pltpu.make_async_copy(w_hbm.at[pl.ds(q * rows, rows)], w.at[pl.ds(q * rows, rows)], wsem.at[q])
        for q in range(4)
    ]
    ids = slots[...]
    place = jnp.where(ids >= 0, ids - (iota(ids.shape, 2) >> 2) * lats, lats)
    tail = jnp.concatenate([(place >> 6).astype(F32), (place & 63).astype(F32)], axis=2)
    aug[:, :, pl.ds(d, 128)] = tail.astype(BF16)
    fill.wait()
    pl.semaphore_wait(barrier, len(column) + len(plane))

    to_layer = []
    for dy, dc in column:
        g = 2 * ring(y, dy) + lax.rem(c + dc, 2)
        to_layer.append(push(aug.at[g], own.at[me], TO_LAYER + 2 * dy + dc, in_column(dy, dc)))
    start(to_layer)
    for load in loads:
        load.start()
    own[me] = aug[me]

    high = dec[...].astype(BF16).astype(F32)
    middle = (dec[...] - high).astype(BF16).astype(F32)
    low = dec[...] - high - middle
    which = iota((16, d), 0)
    decs[...] = jnp.where(
        which == 0, high, jnp.where(which == 1, middle, jnp.where(which == 2, low, 0.0))
    ).astype(BF16)
    norm[...] = jnp.zeros_like(norm)
    mass[...] = jnp.zeros_like(mass)

    def stats(q):
        loads[q].wait()
        per = rows // STAT
        lax.fori_loop(
            q * per, (q + 1) * per, lambda j, _: row_stats(w, decs, enc, inv, bias, norm, j), None
        )

    stats(0)
    arrive(to_layer)

    half = TOK // 2
    first = []
    for k in (1, 3, 2):
        first.append(push(own.at[pl.ds(0, half)], fa.at[z, x], FIRST + k - 1, {X: ring(x, k)}))
        first.append(push(own.at[pl.ds(half, half)], fb.at[x, z], FIRST + 2 + k, {Z: ring(z, k)}))
    start(first)
    fa[z, x] = own[pl.ds(0, half)]
    fb[x, z] = own[pl.ds(half, half)]

    def add_squares(g, acc):
        v = own[g, :, pl.ds(0, d)].astype(F32)
        return acc + v * v

    square = jnp.sum(lax.fori_loop(0, TOK, add_squares, jnp.zeros((TOK, d), F32)))
    squares[here] = jnp.full((8, 128), square, F32)
    square_copies = [
        push(squares.at[here], squares.at[here], SQUARE + 4 * dx + dz, in_plane(dx, dz))
        for dx, dz in plane
    ]
    start(square_copies)
    stats(1)
    arrive(first)

    def beside(h):
        rows = pl.ds(2 * h, 2)
        out = []
        for e, k in enumerate((1, 3)):
            n = AROUND + 2 + 4 * h + 2 * e
            out.append(push(fa.at[z, :, rows], fa.at[z, :, rows], n, {Z: ring(z, k)}))
            out.append(push(fb.at[x, :, rows], fb.at[x, :, rows], n + 1, {X: ring(x, k)}))
        return out

    across = [
        push(fa.at[z], fa.at[z], AROUND, {Z: ring(z, 2)}),
        push(fb.at[x], fb.at[x], AROUND + 1, {X: ring(x, 2)}),
    ]
    beside_a, beside_b = beside(0), beside(1)
    start(beside_a)
    sent.extend(across + beside_b)
    stats(2)
    stats(3)
    places[...] = seed_places(seed_tokens, x, z)
    arrive(square_copies)
    scale = lax.rsqrt(jnp.sum(squares[...], axis=0)[0:1, 0:1] / (tokens * d))

    pick_row = iota((128, 512), 0)
    pick_slot = (iota((128, 512), 1) >> 7) + 4 * here
    pick = jnp.where(pick_row == pick_slot, 64.0, 0.0) + jnp.where(pick_row == pick_slot + 64, 1.0, 0.0)
    pick = pick.astype(BF16)

    def near_share(h):
        devices = ({Z: ring(z, 1)}, {Z: ring(z, 3)}, {X: ring(x, 1)}, {X: ring(x, 3)})
        return [
            push(part.at[1 + 2 * h, pl.ds(e * 64, 64)], near_in.at[h, e], NEAR + 4 * h + e, device)
            for e, device in enumerate(devices)
        ]

    near_a, near_b = near_share(0), near_share(1)
    far = [
        push(part.at[2, pl.ds(0, 128)], fara, FAR, {Z: ring(z, 2)}),
        push(part.at[2, pl.ds(128, 128)], farb, FAR + 1, {X: ring(x, 2)}),
    ]
    sent.extend(far + near_a + near_b)

    def decode(step, source):
        @pl.loop(0, d // COLS)
        def _(n):
            at = pl.ds(pl.multiple_of(n * COLS, COLS), COLS)
            v = jnp.dot(source[...], w[:, at], preferred_element_type=F32)
            part[step, :, at] = v.astype(BF16)

    def block(step, _):
        close = step % 2

        @pl.when(step == 1)
        def _():
            arrive(beside_a)

        @pl.when(step == 2)
        def _():
            arrive(across)

        @pl.when(step == 3)
        def _():
            arrive(beside_b)

        lane = iota((16, 8, 128), 2)
        for h, buf, at in ((0, fa, z), (1, fb, x)):

            def chunk(m, cols):
                away = (1 - close) * step + close * (1 + m // 4 * 2)
                index = (1 - close) * (m // 2) + close * (m % 4)
                low = (1 - close) * (m % 2 * 2) + close * (step - 1)
                v = buf[ring(at, away), index, pl.ds(low, 2), :, cols]
                return v.astype(F32).reshape(16, cols.size)

            def normalize(m, _, h=h, chunk=chunk):
                v = chunk(m, pl.ds(0, d)) * scale
                nf[step, pl.ds(h * 128 + m * 16, 16), :] = v.astype(BF16)

            lax.fori_loop(0, 8, normalize, None)
            tails = [chunk(m, pl.ds(d, 128)) for m in range(8)]
            tails = jnp.concatenate(tails, axis=0).astype(BF16)
            found = jnp.dot(tails, pick, preferred_element_type=F32).astype(jnp.int32)
            fields = [jnp.zeros((16, 8, 128), jnp.int32) for _ in range(lats // TILE)]
            for s in range(4):
                v = found[:, s * 128 : (s + 1) * 128].reshape(16, 8, 128)
                one = jnp.where((v & 127) == lane, jnp.int32(1) << (((v >> 7) & 7) << 2), 0)
                fields = [f + jnp.where(v >> 10 == j, one, 0) for j, f in enumerate(fields)]
            for j, f in enumerate(fields):
                bits[j, pl.ds(16 * h, 16)] = f

        def between():
            @pl.when(step == 0)
            def _():
                for copy in across:
                    copy.start()

        mine = jnp.minimum(step, 1)
        encode(nf.at[step], w, bits, inv, bias, mass, coef.at[mine], p, between)

        @pl.when(step == 1)
        def _():
            for copy in beside_b:
                copy.start()

        @pl.when(step > 0)
        def _():
            decode(step, coef.at[1])

        @pl.when(step == 1)
        def _():
            for copy in near_a:
                copy.start()

        @pl.when(step == 2)
        def _():
            for copy in far:
                copy.start()

        @pl.when(step == 3)
        def _():
            for copy in near_b:
                copy.start()

    lax.fori_loop(0, 4, block, None)

    hot = one_hot(places[...], tokens)

    @pl.loop(0, d // 512)
    def _(n):
        at = pl.ds(pl.multiple_of(n * 512, 512), 512)
        others = part[1:, :, at].reshape(3 * BLOCK, 512)
        picked[:, at] = jnp.dot(hot[:, BLOCK:], others, preferred_element_type=F32)

    decode(0, coef.at[0])

    def combine(h):
        for i in range(4):
            at, in_h = pl.ds(i * HALF + h * 16, 16), pl.ds(i * 16, 16)
            for to, got, lo, e in ((sa, fara, 0, 0), (sb, farb, 128, 2)):
                v = part[0, pl.ds(lo + i * HALF + h * 16, 16), :].astype(F32) + got[at, :].astype(F32)
                v = v + near_in[h, e, in_h, :].astype(F32) + near_in[h, e + 1, in_h, :].astype(F32)
                to[h, i] = v.astype(BF16)
        copies = []
        for k in (2, 1, 3):
            n = LAST + 6 * h + k - 1
            copies.append(push(sa.at[h, ring(x, k)], ta.at[h, k - 1], n, {X: ring(x, k)}))
            copies.append(push(sb.at[h, ring(z, k)], tb.at[h, k - 1], n + 3, {Z: ring(z, k)}))
        start(copies)
        return copies

    arrive(far)
    arrive(near_a)
    last = [combine(0)]

    @pl.loop(0, d // 512)
    def _(n):
        at = pl.ds(pl.multiple_of(n * 512, 512), 512)
        v = jnp.dot(hot[:, :BLOCK], part[0, :, at], preferred_element_type=F32) + picked[:, at]
        seeds[:, :, :, :, at] = v.reshape(4, 2, 4, RES, 512).astype(BF16)

    seed_copies = []
    for k in (2, 1, 3):
        seed_copies.append(push(seeds.at[k, 0], rsa.at[k - 1], SEEDS + k - 1, {Z: ring(z, k)}))
        seed_copies.append(push(seeds.at[k, 1], rsb.at[k - 1], SEEDS + 2 + k, {X: ring(x, k)}))
    arrive(near_b)
    last.append(combine(1))
    start(seed_copies)

    def add_tokens(q, acc):
        for k in range(4):
            acc = acc + nf[k, pl.ds(q * 16, 16), :].astype(F32)
        return acc

    sums = lax.fori_loop(0, BLOCK // 16, add_tokens, jnp.zeros((16, d), F32))
    means = jnp.sum(sums, axis=0, keepdims=True) / tokens
    my_places = jnp.concatenate(
        [places[pl.ds(x * RES, RES), :], places[pl.ds(4 * RES + z * RES, RES), :]], axis=0
    )
    seed_feats = jnp.dot(
        one_hot(my_places, tokens), nf[...].reshape(tokens, d), preferred_element_type=F32
    )
    norm_sum = jnp.sum(norm[...]) / 8.0

    def back(g):
        device = {Y: g // 2 + 0 * y, C: g % 2 + 0 * c}
        return pltpu.make_async_remote_copy(
            src_ref=rec.at[g], dst_ref=recon.at[me], send_sem=send.at[BACK + g],
            recv_sem=recv.at[BACK + me], device_id=device, device_id_type=MESH,
        )

    def elsewhere(g, act):
        @pl.when(me != g)
        def _():
            act()

    numerator = denominator = 0.0
    for h in range(2):
        arrive(last[h])
        for mine_sum, got, g, lo in (
            (sa.at[h, x], ta, 2 * h, x * HALF),
            (sb.at[h, z], tb, half + 2 * h, 128 + z * HALF),
        ):
            v = mine_sum[...].astype(F32)
            for k in range(3):
                v = v + got[h, k].astype(F32)
            v = v + dec[...]
            rec[pl.ds(g, 2)] = v.reshape(2, TOK, d).astype(BF16)
            for e in (g, g + 1):
                elsewhere(e, lambda e=e: back(e).start())
            feats = nf[0, pl.ds(lo + 16 * h, 16), :].astype(F32)
            e, m = feats - v, feats - means
            numerator = numerator + jnp.sum(e * e)
            denominator = denominator + jnp.sum(m * m)
    recon[me] = rec[me]
    kind = iota((8, 128), 0)
    finals[here] = jnp.where(kind == 0, numerator, jnp.where(kind == 1, denominator, norm_sum))
    final_copies = [
        push(finals.at[here], finals.at[here], FINAL + 4 * dx + dz, in_plane(dx, dz)) for dx, dz in plane
    ]
    start(final_copies)
    arrive(seed_copies)

    def add_seeds(q, _):
        for to, got, h in ((ssa, rsa, 0), (ssb, rsb, 1)):
            v = seeds[0, h, q].astype(F32)
            for k in range(3):
                v = v + got[k, q].astype(F32)
            to[q] = v.astype(BF16)

    lax.fori_loop(0, 4, add_seeds, None)
    last_seeds = []
    for k in (1, 3, 2):
        last_seeds.append(push(ssa.at[ring(x, k)], tsa.at[k - 1], LAST_SEEDS + k - 1, {X: ring(x, k)}))
        last_seeds.append(push(ssb.at[ring(z, k)], tsb.at[k - 1], LAST_SEEDS + 2 + k, {Z: ring(z, k)}))
    start(last_seeds)

    lanes = lats // 128
    gone = dead[...] - here * lats
    at_row = jnp.where(iota((lanes, gone.shape[1]), 0) == gone >> 7, 1.0, 0.0).astype(BF16)
    at_lane = jnp.where(iota((128, gone.shape[1]), 0) == (gone & 127), 1.0, 0.0).astype(BF16)
    hits = lax.dot_general(at_row, at_lane, NT, preferred_element_type=F32)
    new_bias[...] = jnp.where(hits > 0.5, 0.0, enc[...])
    mass_out[...] = jnp.sum(mass[...], axis=1)

    arrive(last_seeds)
    estimates = []
    for mine_sum, got in ((ssa.at[x], tsa), (ssb.at[z], tsb)):
        v = mine_sum[...].astype(F32)
        for k in range(3):
            v = v + got[k].astype(F32)
        estimates.append(v + dec[...])
    errors = seed_feats - jnp.concatenate(estimates, axis=0)
    seed_norm = jnp.sqrt(jnp.sum(errors * errors, axis=1, keepdims=True) + 1e-06)
    unit = errors / seed_norm
    arrive(final_copies)
    total = jnp.sum(finals[...], axis=0)
    ratio = total[0:1, :] / total[1:2, :]
    unexplained[0] = ratio[0, 0]
    new_rows[...] = (unit * (total[2:3, 0:1] / (lats * 16))).astype(BF16)
    for g in range(TOK):
        def settle(g=g):
            pltpu.make_async_remote_copy(
                src_ref=rec.at[g], dst_ref=recon.at[g], send_sem=send.at[BACK + g],
                recv_sem=recv.at[BACK + g], device_id={Y: ring(y, 1)}, device_id_type=MESH,
            ).wait()

        elsewhere(g, settle)
    for copy in sent:
        copy.wait_send()


def hand_over(*refs):
    count = len(refs) // 2
    refs[count][0] = refs[0][0]
    for i in range(1, count):
        refs[count + i][...] = refs[i][...]


def handed_over(*arrays):
    specs = [pl.BlockSpec(memory_space=pltpu.SMEM)]
    specs += [pl.BlockSpec(memory_space=pltpu.VMEM)] * (len(arrays) - 1)
    return pl.pallas_call(
        hand_over,
        out_shape=tuple(jax.ShapeDtypeStruct(a.shape, a.dtype) for a in arrays),
        in_specs=specs,
        out_specs=tuple(specs),
        name="hand_over",
    )(*arrays)


def fused(residuals, slots, rows, dec, enc, dead, seed_tokens):
    lats, d = rows.shape
    wide = d + 128
    lanes = lats // 128
    vmem = pl.BlockSpec(memory_space=pltpu.VMEM)
    hbm = pl.BlockSpec(memory_space=pl.ANY)
    half = TOK // 2
    scratch = [
        ((lats, d), BF16),
        ((TOK, TOK, wide), BF16),
        ((TOK, TOK, wide), BF16),
        ((4, 4, half, TOK, wide), BF16),
        ((4, 4, half, TOK, wide), BF16),
        ((4, BLOCK, d), BF16),
        ((lats // TILE, BLOCK // 8, 8, 128), jnp.int32),
        ((2, BLOCK, lats), BF16),
        ((2, BLOCK, TILE), F32),
        ((4, BLOCK, d), BF16),
        ((128, d), BF16),
        ((128, d), BF16),
        ((2, 4, 64, d), BF16),
        ((seed_tokens.shape[1], d), F32),
        ((4, 2, 4, RES, d), BF16),
        ((3, 4, RES, d), BF16),
        ((3, 4, RES, d), BF16),
        ((2, 4, HALF // 2, d), BF16),
        ((2, 4, HALF // 2, d), BF16),
        ((2, 3, HALF // 2, d), BF16),
        ((2, 3, HALF // 2, d), BF16),
        ((4, RES, d), BF16),
        ((4, RES, d), BF16),
        ((3, RES, d), BF16),
        ((3, RES, d), BF16),
        ((16, 8, 128), F32),
        ((16, 8, 128), F32),
        ((lanes, 8, 128), F32),
        ((lanes, 8, 128), F32),
        ((8, STAT), F32),
        ((lanes, 8, 128), F32),
        ((16, d), BF16),
        ((seed_tokens.shape[1], 128), F32),
        ((TOK, TOK, d), BF16),
    ]
    return pl.pallas_call(
        kernel,
        out_shape=(
            jax.ShapeDtypeStruct((TOK, TOK, d), BF16),
            jax.ShapeDtypeStruct((1,), F32),
            jax.ShapeDtypeStruct((lanes, 128), F32),
            jax.ShapeDtypeStruct((2 * RES, d), BF16),
            jax.ShapeDtypeStruct((lanes, 128), F32),
        ),
        in_specs=[hbm, vmem, hbm, vmem, vmem, vmem, vmem],
        out_specs=(vmem, pl.BlockSpec(memory_space=pltpu.SMEM), vmem, vmem, vmem),
        scratch_shapes=[pltpu.VMEM(*s) for s in scratch]
        + [
            pltpu.SemaphoreType.DMA((COUNT,)),
            pltpu.SemaphoreType.DMA((COUNT,)),
            pltpu.SemaphoreType.DMA((4,)),
            pltpu.SemaphoreType.DMA((1,)),
        ],
        compiler_params=pltpu.CompilerParams(
            collective_id=0, has_side_effects=True, vmem_limit_bytes=60 * 2**20
        ),
        name="sae",
    )(residuals, slots, rows, dec, enc.reshape(lanes, 128), dead, seed_tokens)


def body(residuals, topk_slots, dictionary, enc_bias, dec_bias, dead_ids, seed_tokens):
    recon, unexplained, mass, new_rows, new_bias = fused(
        residuals, topk_slots, dictionary[0], dec_bias, enc_bias, dead_ids, seed_tokens
    )
    unexplained, recon, mass, new_rows, new_bias = handed_over(
        unexplained, recon, mass, new_rows, new_bias
    )
    return (recon, unexplained, mass.reshape(1, -1), new_rows[None], new_bias.reshape(1, -1))


def solution(mesh):
    split = Mesh(mesh.devices.reshape(4, 2, 4, 4), (Y, C, X, Z))
    placed = (
        P(None, LAYER_LAT, None),
        P(None, LAYER_LAT, None),
        P(LAYER, LAT, None),
        P(LAYER, LAT),
        P(LAYER, None),
        P(LAYER, None),
        P(LAYER, None),
    )
    return jax.shard_map(
        body,
        mesh=split,
        in_specs=placed,
        out_specs=(
            P(None, LAYER_LAT, None),
            P(LAYER),
            P(LAYER, LAT),
            P(LAYER, LAT, None),
            P(LAYER, LAT),
        ),
        check_vma=False,
    )
```

```python
import jax
import jax.numpy as jnp
from jax import lax
from jax.experimental import pallas as pl
from jax.experimental.pallas import tpu as pltpu
from jax.sharding import Mesh
from jax.sharding import PartitionSpec as P

Y, C, X, Z = "layer_0", "layer_1", "lat_0", "lat_1"
LAT = (X, Z)
LAYER = (Y, C)
LAYER_LAT = (Y, C, X, Z)
MESH = pl.DeviceIdType.MESH
NT = (((1,), (1,)), ((), ()))
F32 = jnp.float32
BF16 = jnp.bfloat16
TILE = 1024
STAT = 512
COLS = 2048
TOK = 8
HALF = 32
BLOCK = 256
RES = 8
GROUPS = TILE // 128

TO_LAYER, FIRST, AROUND, SQUARE, FAR, NEAR, SEEDS, LAST, LAST_SEEDS, FINAL, BACK, COUNT = (
    0, 8, 14, 24, 40, 42, 50, 56, 68, 74, 90, 98
)


def row_stats(w, decs, enc, inv, bias, norm, j):
    sq = None
    tile = pl.ds(j * STAT, STAT)
    for g in range(w.shape[1] // 128):
        piece = w[tile, g * 128 : (g + 1) * 128].astype(F32)
        a = piece * piece
        sq = a if sq is None else sq + a
    ones = jnp.ones((8, 128), F32)
    total = lax.dot_general(
        ones, sq, NT, precision=lax.Precision.HIGHEST, preferred_element_type=F32
    )
    parts = lax.dot_general(decs[...], w[tile, :], NT, preferred_element_type=F32)
    shift = jnp.sum(parts, axis=0, keepdims=True)
    n = jnp.sqrt(total + 1e-06)
    norm[...] += n
    iv = 1.0 / n
    for g in range(STAT // 128):
        at = slice(g * 128, (g + 1) * 128)
        row = j * (STAT // 128) + g
        inv[row] = iv[:, at]
        bias[row] = enc[pl.ds(row, 1), :] - shift[:, at] * iv[:, at]


def encode(feats, w, bits, inv, bias, mass, coef, p, between):
    tiles = w.shape[0] // TILE

    def product(j):
        p[j % 2] = lax.dot_general(
            feats[...], w[pl.ds(j * TILE, TILE), :], NT, preferred_element_type=F32
        )

    def activity(j):
        for g in range(GROUPS):
            row = j * GROUPS + g
            iv = inv[row]
            pre = p[j % 2, :, g * 128 : (g + 1) * 128].reshape(BLOCK // 8, 8, 128)
            count = ((bits[j] >> (4 * g)) & 15).astype(F32)
            total = jnp.maximum(pre * iv + bias[row], 0.0) * count
            mass[row] += jnp.sum(total, axis=0)
            coef[:, row * 128 : (row + 1) * 128] = (total * iv).reshape(BLOCK, 128).astype(BF16)

    product(0)
    for j in range(1, tiles):
        product(j)
        activity(j - 1)
        if j == 3:
            between()
    activity(tiles - 1)


def iota(shape, dim):
    return lax.broadcasted_iota(jnp.int32, shape, dim)


def seed_places(seeds, x, z):
    n = seeds[...]
    home, g, t = (n >> 3) & 15, n >> 7, n & 7
    xi, zi = home >> 2, home & 3
    is_a = g < 4
    far = jnp.where(is_a, zi - z, xi - x) & 3
    index = jnp.where(is_a, xi, zi)
    odd = (far & 1) == 1
    step = jnp.where(odd, 1 + ((g & 3) >> 1 << 1), far)
    inside = jnp.where(
        odd, (far >> 1) * 64 + index * 16 + (g & 1) * TOK, index * HALF + (g & 3) * TOK
    )
    place = step * BLOCK + jnp.where(is_a, 0, 128) + inside + t
    size = seeds.shape[1]
    row, col = iota((size, size), 0), iota((size, size), 1)
    k, h, i = row >> 6, (row >> 5) & 1, (row >> 3) & 3
    xr = jnp.where(h == 0, i, (x + k) & 3)
    zr = jnp.where(h == 0, (z + k) & 3, i)
    match = col == (xr * 4 + zr) * 16 + h * RES + (row & 7)
    ones = jnp.ones((size, 128), BF16)

    def column(v):
        kept = jnp.where(match, v.astype(F32), 0.0).astype(BF16)
        return jnp.dot(kept, ones, preferred_element_type=F32)

    return column(place >> 5) * 32.0 + column(place & 31)


def one_hot(places, count):
    spots = iota(places.shape, 1).astype(F32)
    return jnp.concatenate(
        [jnp.where(places - q * 128.0 == spots, 1.0, 0.0) for q in range(count // 128)], axis=1
    ).astype(BF16)


def kernel(
    res, slots, w_hbm, dec, enc, dead, seed_tokens,
    recon, unexplained, mass_out, new_rows, new_bias,
    w, aug, own, fa, fb, nf, bits, coef, p, part, fara, farb, near_in, picked, seeds, rsa, rsb,
    sa, sb, ta, tb, ssa, ssb, tsa, tsb, squares, finals, inv, bias, norm, mass, decs, places, rec,
    send, recv, wsem, osem,
):
    d = w.shape[1]
    lats = w.shape[0]
    y, c, x, z = (lax.axis_index(a) for a in (Y, C, X, Z))
    me = 2 * y + c
    here = 4 * x + z
    tokens = 4 * BLOCK

    def ring(at, step):
        return lax.rem(at + step, 4)

    def push(src, dst, n, device):
        return pltpu.make_async_remote_copy(
            src_ref=src, dst_ref=dst, send_sem=send.at[n], recv_sem=recv.at[n],
            device_id=device, device_id_type=MESH,
        )

    def local(src, dst, n):
        return pltpu.make_async_copy(src, dst, osem.at[n])

    sent = []

    def start(copies):
        for copy in copies:
            copy.start()
        sent.extend(copies)

    def arrive(copies):
        for copy in copies:
            copy.wait_recv()

    column = [(dy, dc) for dy in range(4) for dc in range(2) if dy or dc]
    plane = [(dx, dz) for dx in range(4) for dz in range(4) if dx or dz]

    def in_column(dy, dc):
        return {Y: ring(y, dy), C: lax.rem(c + dc, 2)}

    def in_plane(dx, dz):
        return {X: ring(x, dx), Z: ring(z, dz)}

    barrier = pltpu.get_barrier_semaphore()
    for dy, dc in column:
        pl.semaphore_signal(barrier, inc=1, device_id=in_column(dy, dc), device_id_type=MESH)
    for dx, dz in plane:
        pl.semaphore_signal(barrier, inc=1, device_id=in_plane(dx, dz), device_id_type=MESH)

    fill = local(res, aug.at[:, :, pl.ds(0, d)], 0)
    fill.start()
    rows = lats // 4
    loads = [
        pltpu.make_async_copy(w_hbm.at[pl.ds(q * rows, rows)], w.at[pl.ds(q * rows, rows)], wsem.at[q])
        for q in range(4)
    ]
    ids = slots[...]
    place = jnp.where(ids >= 0, ids - (iota(ids.shape, 2) >> 2) * lats, lats)
    tail = jnp.concatenate([(place >> 6).astype(F32), (place & 63).astype(F32)], axis=2)
    aug[:, :, pl.ds(d, 128)] = tail.astype(BF16)
    fill.wait()
    pl.semaphore_wait(barrier, len(column) + len(plane))

    to_layer = []
    for dy, dc in column:
        g = 2 * ring(y, dy) + lax.rem(c + dc, 2)
        to_layer.append(push(aug.at[g], own.at[me], TO_LAYER + 2 * dy + dc, in_column(dy, dc)))
    start(to_layer)
    for load in loads:
        load.start()
    own[me] = aug[me]

    high = dec[...].astype(BF16).astype(F32)
    middle = (dec[...] - high).astype(BF16).astype(F32)
    low = dec[...] - high - middle
    which = iota((16, d), 0)
    decs[...] = jnp.where(
        which == 0, high, jnp.where(which == 1, middle, jnp.where(which == 2, low, 0.0))
    ).astype(BF16)
    norm[...] = jnp.zeros_like(norm)
    mass[...] = jnp.zeros_like(mass)

    def stats(q):
        loads[q].wait()
        per = rows // STAT
        lax.fori_loop(
            q * per, (q + 1) * per, lambda j, _: row_stats(w, decs, enc, inv, bias, norm, j), None
        )

    stats(0)
    arrive(to_layer)

    half = TOK // 2
    first = []
    for k in (1, 3, 2):
        first.append(push(own.at[pl.ds(0, half)], fa.at[z, x], FIRST + k - 1, {X: ring(x, k)}))
        first.append(push(own.at[pl.ds(half, half)], fb.at[x, z], FIRST + 2 + k, {Z: ring(z, k)}))
    start(first)
    fa[z, x] = own[pl.ds(0, half)]
    fb[x, z] = own[pl.ds(half, half)]

    def add_squares(g, acc):
        v = own[g, :, pl.ds(0, d)].astype(F32)
        return acc + v * v

    square = jnp.sum(lax.fori_loop(0, TOK, add_squares, jnp.zeros((TOK, d), F32)))
    squares[here] = jnp.full((8, 128), square, F32)
    square_copies = [
        push(squares.at[here], squares.at[here], SQUARE + 4 * dx + dz, in_plane(dx, dz))
        for dx, dz in plane
    ]
    start(square_copies)
    for q in (1, 2, 3):
        stats(q)
    places[...] = seed_places(seed_tokens, x, z)
    arrive(first)

    def beside(h):
        rows = pl.ds(2 * h, 2)
        out = []
        for e, k in enumerate((1, 3)):
            n = AROUND + 2 + 4 * h + 2 * e
            out.append(push(fa.at[z, :, rows], fa.at[z, :, rows], n, {Z: ring(z, k)}))
            out.append(push(fb.at[x, :, rows], fb.at[x, :, rows], n + 1, {X: ring(x, k)}))
        return out

    across = [
        push(fa.at[z], fa.at[z], AROUND, {Z: ring(z, 2)}),
        push(fb.at[x], fb.at[x], AROUND + 1, {X: ring(x, 2)}),
    ]
    beside_a, beside_b = beside(0), beside(1)
    start(beside_a)
    sent.extend(across + beside_b)
    arrive(square_copies)
    scale = lax.rsqrt(jnp.sum(squares[...], axis=0)[0:1, 0:1] / (tokens * d))

    pick_row = iota((128, 512), 0)
    pick_slot = (iota((128, 512), 1) >> 7) + 4 * here
    pick = jnp.where(pick_row == pick_slot, 64.0, 0.0) + jnp.where(pick_row == pick_slot + 64, 1.0, 0.0)
    pick = pick.astype(BF16)

    def near_share(h):
        devices = ({Z: ring(z, 1)}, {Z: ring(z, 3)}, {X: ring(x, 1)}, {X: ring(x, 3)})
        return [
            push(part.at[1 + 2 * h, pl.ds(e * 64, 64)], near_in.at[h, e], NEAR + 4 * h + e, device)
            for e, device in enumerate(devices)
        ]

    near_a, near_b = near_share(0), near_share(1)
    far = [
        push(part.at[2, pl.ds(0, 128)], fara, FAR, {Z: ring(z, 2)}),
        push(part.at[2, pl.ds(128, 128)], farb, FAR + 1, {X: ring(x, 2)}),
    ]
    sent.extend(far + near_a + near_b)

    def decode(step, source):
        @pl.loop(0, d // COLS)
        def _(n):
            at = pl.ds(pl.multiple_of(n * COLS, COLS), COLS)
            v = jnp.dot(source[...], w[:, at], preferred_element_type=F32)
            part[step, :, at] = v.astype(BF16)

    def block(step, _):
        close = step % 2

        @pl.when(step == 1)
        def _():
            arrive(beside_a)

        @pl.when(step == 2)
        def _():
            arrive(across)

        @pl.when(step == 3)
        def _():
            arrive(beside_b)

        lane = iota((16, 8, 128), 2)
        for h, buf, at in ((0, fa, z), (1, fb, x)):

            def chunk(m, cols):
                away = (1 - close) * step + close * (1 + m // 4 * 2)
                index = (1 - close) * (m // 2) + close * (m % 4)
                low = (1 - close) * (m % 2 * 2) + close * (step - 1)
                v = buf[ring(at, away), index, pl.ds(low, 2), :, cols]
                return v.astype(F32).reshape(16, cols.size)

            def normalize(m, _, h=h, chunk=chunk):
                v = chunk(m, pl.ds(0, d)) * scale
                nf[step, pl.ds(h * 128 + m * 16, 16), :] = v.astype(BF16)

            lax.fori_loop(0, 8, normalize, None)
            tails = [chunk(m, pl.ds(d, 128)) for m in range(8)]
            tails = jnp.concatenate(tails, axis=0).astype(BF16)
            found = jnp.dot(tails, pick, preferred_element_type=F32).astype(jnp.int32)
            fields = [jnp.zeros((16, 8, 128), jnp.int32) for _ in range(lats // TILE)]
            for s in range(4):
                v = found[:, s * 128 : (s + 1) * 128].reshape(16, 8, 128)
                one = jnp.where((v & 127) == lane, jnp.int32(1) << (((v >> 7) & 7) << 2), 0)
                fields = [f + jnp.where(v >> 10 == j, one, 0) for j, f in enumerate(fields)]
            for j, f in enumerate(fields):
                bits[j, pl.ds(16 * h, 16)] = f

        def between():
            @pl.when(step == 0)
            def _():
                for copy in across:
                    copy.start()

        mine = jnp.minimum(step, 1)
        encode(nf.at[step], w, bits, inv, bias, mass, coef.at[mine], p, between)

        @pl.when(step == 1)
        def _():
            for copy in beside_b:
                copy.start()

        @pl.when(step > 0)
        def _():
            decode(step, coef.at[1])

        @pl.when(step == 1)
        def _():
            for copy in near_a:
                copy.start()

        @pl.when(step == 2)
        def _():
            for copy in far:
                copy.start()

        @pl.when(step == 3)
        def _():
            for copy in near_b:
                copy.start()

    lax.fori_loop(0, 4, block, None)

    hot = one_hot(places[...], tokens)

    @pl.loop(0, d // 1024)
    def _(n):
        at = pl.ds(pl.multiple_of(n * 1024, 1024), 1024)
        others = part[1:, :, at].reshape(3 * BLOCK, 1024)
        picked[:, at] = jnp.dot(hot[:, BLOCK:], others, preferred_element_type=F32)

    decode(0, coef.at[0])

    def combine(h):
        for i in range(4):
            at, in_h = pl.ds(i * HALF + h * 16, 16), pl.ds(i * 16, 16)
            for to, got, lo, e in ((sa, fara, 0, 0), (sb, farb, 128, 2)):
                v = part[0, pl.ds(lo + i * HALF + h * 16, 16), :].astype(F32) + got[at, :].astype(F32)
                v = v + near_in[h, e, in_h, :].astype(F32) + near_in[h, e + 1, in_h, :].astype(F32)
                to[h, i] = v.astype(BF16)
        copies = []
        for k in (2, 1, 3):
            n = LAST + 6 * h + k - 1
            copies.append(push(sa.at[h, ring(x, k)], ta.at[h, k - 1], n, {X: ring(x, k)}))
            copies.append(push(sb.at[h, ring(z, k)], tb.at[h, k - 1], n + 3, {Z: ring(z, k)}))
        start(copies)
        return copies

    arrive(far)
    arrive(near_a)
    last = [combine(0)]

    @pl.loop(0, d // 1024)
    def _(n):
        at = pl.ds(pl.multiple_of(n * 1024, 1024), 1024)
        v = jnp.dot(hot[:, :BLOCK], part[0, :, at], preferred_element_type=F32) + picked[:, at]
        seeds[:, :, :, :, at] = v.reshape(4, 2, 4, RES, 1024).astype(BF16)

    seed_copies = []
    for k in (2, 1, 3):
        seed_copies.append(push(seeds.at[k, 0], rsa.at[k - 1], SEEDS + k - 1, {Z: ring(z, k)}))
        seed_copies.append(push(seeds.at[k, 1], rsb.at[k - 1], SEEDS + 2 + k, {X: ring(x, k)}))
    arrive(near_b)
    last.append(combine(1))
    start(seed_copies)

    def add_tokens(q, acc):
        for k in range(4):
            acc = acc + nf[k, pl.ds(q * 16, 16), :].astype(F32)
        return acc

    sums = lax.fori_loop(0, BLOCK // 16, add_tokens, jnp.zeros((16, d), F32))
    means = jnp.sum(sums, axis=0, keepdims=True) / tokens
    my_places = jnp.concatenate(
        [places[pl.ds(x * RES, RES), :], places[pl.ds(4 * RES + z * RES, RES), :]], axis=0
    )
    seed_feats = jnp.dot(
        one_hot(my_places, tokens), nf[...].reshape(tokens, d), preferred_element_type=F32
    )
    norm_sum = jnp.sum(norm[...]) / 8.0

    def back(g):
        device = {Y: g // 2 + 0 * y, C: g % 2 + 0 * c}
        return pltpu.make_async_remote_copy(
            src_ref=rec.at[g], dst_ref=recon.at[me], send_sem=send.at[BACK + g],
            recv_sem=recv.at[BACK + me], device_id=device, device_id_type=MESH,
        )

    def elsewhere(g, act):
        @pl.when(me != g)
        def _():
            act()

    numerator = denominator = 0.0
    for h in range(2):
        arrive(last[h])
        for mine_sum, got, g, lo in (
            (sa.at[h, x], ta, 2 * h, x * HALF),
            (sb.at[h, z], tb, half + 2 * h, 128 + z * HALF),
        ):
            v = mine_sum[...].astype(F32)
            for k in range(3):
                v = v + got[h, k].astype(F32)
            v = v + dec[...]
            rec[pl.ds(g, 2)] = v.reshape(2, TOK, d).astype(BF16)
            for e in (g, g + 1):
                elsewhere(e, lambda e=e: back(e).start())
            feats = nf[0, pl.ds(lo + 16 * h, 16), :].astype(F32)
            e, m = feats - v, feats - means
            numerator = numerator + jnp.sum(e * e)
            denominator = denominator + jnp.sum(m * m)
    recon[me] = rec[me]
    kind = iota((8, 128), 0)
    finals[here] = jnp.where(kind == 0, numerator, jnp.where(kind == 1, denominator, norm_sum))
    final_copies = [
        push(finals.at[here], finals.at[here], FINAL + 4 * dx + dz, in_plane(dx, dz)) for dx, dz in plane
    ]
    start(final_copies)
    arrive(seed_copies)

    def add_seeds(q, _):
        for to, got, h in ((ssa, rsa, 0), (ssb, rsb, 1)):
            v = seeds[0, h, q].astype(F32)
            for k in range(3):
                v = v + got[k, q].astype(F32)
            to[q] = v.astype(BF16)

    lax.fori_loop(0, 4, add_seeds, None)
    last_seeds = []
    for k in (1, 3, 2):
        last_seeds.append(push(ssa.at[ring(x, k)], tsa.at[k - 1], LAST_SEEDS + k - 1, {X: ring(x, k)}))
        last_seeds.append(push(ssb.at[ring(z, k)], tsb.at[k - 1], LAST_SEEDS + 2 + k, {Z: ring(z, k)}))
    start(last_seeds)

    lanes = lats // 128
    gone = dead[...] - here * lats
    at_row = jnp.where(iota((lanes, gone.shape[1]), 0) == gone >> 7, 1.0, 0.0).astype(BF16)
    at_lane = jnp.where(iota((128, gone.shape[1]), 0) == (gone & 127), 1.0, 0.0).astype(BF16)
    hits = lax.dot_general(at_row, at_lane, NT, preferred_element_type=F32)
    new_bias[...] = jnp.where(hits > 0.5, 0.0, enc[...])
    mass_out[...] = jnp.sum(mass[...], axis=1)

    arrive(last_seeds)
    estimates = []
    for mine_sum, got in ((ssa.at[x], tsa), (ssb.at[z], tsb)):
        v = mine_sum[...].astype(F32)
        for k in range(3):
            v = v + got[k].astype(F32)
        estimates.append(v + dec[...])
    errors = seed_feats - jnp.concatenate(estimates, axis=0)
    seed_norm = jnp.sqrt(jnp.sum(errors * errors, axis=1, keepdims=True) + 1e-06)
    unit = errors / seed_norm
    arrive(final_copies)
    total = jnp.sum(finals[...], axis=0)
    ratio = total[0:1, :] / total[1:2, :]
    unexplained[0] = ratio[0, 0]
    new_rows[...] = (unit * (total[2:3, 0:1] / (lats * 16))).astype(BF16)
    for g in range(TOK):
        def settle(g=g):
            pltpu.make_async_remote_copy(
                src_ref=rec.at[g], dst_ref=recon.at[g], send_sem=send.at[BACK + g],
                recv_sem=recv.at[BACK + g], device_id={Y: ring(y, 1)}, device_id_type=MESH,
            ).wait()

        elsewhere(g, settle)
    for copy in sent:
        copy.wait_send()


def hand_over(*refs):
    count = len(refs) // 2
    refs[count][0] = refs[0][0]
    for i in range(1, count):
        refs[count + i][...] = refs[i][...]


def handed_over(*arrays):
    specs = [pl.BlockSpec(memory_space=pltpu.SMEM)]
    specs += [pl.BlockSpec(memory_space=pltpu.VMEM)] * (len(arrays) - 1)
    return pl.pallas_call(
        hand_over,
        out_shape=tuple(jax.ShapeDtypeStruct(a.shape, a.dtype) for a in arrays),
        in_specs=specs,
        out_specs=tuple(specs),
        name="hand_over",
    )(*arrays)


def fused(residuals, slots, rows, dec, enc, dead, seed_tokens):
    lats, d = rows.shape
    wide = d + 128
    lanes = lats // 128
    vmem = pl.BlockSpec(memory_space=pltpu.VMEM)
    hbm = pl.BlockSpec(memory_space=pl.ANY)
    half = TOK // 2
    scratch = [
        ((lats, d), BF16),
        ((TOK, TOK, wide), BF16),
        ((TOK, TOK, wide), BF16),
        ((4, 4, half, TOK, wide), BF16),
        ((4, 4, half, TOK, wide), BF16),
        ((4, BLOCK, d), BF16),
        ((lats // TILE, BLOCK // 8, 8, 128), jnp.int32),
        ((2, BLOCK, lats), BF16),
        ((2, BLOCK, TILE), F32),
        ((4, BLOCK, d), BF16),
        ((128, d), BF16),
        ((128, d), BF16),
        ((2, 4, 64, d), BF16),
        ((seed_tokens.shape[1], d), F32),
        ((4, 2, 4, RES, d), BF16),
        ((3, 4, RES, d), BF16),
        ((3, 4, RES, d), BF16),
        ((2, 4, HALF // 2, d), BF16),
        ((2, 4, HALF // 2, d), BF16),
        ((2, 3, HALF // 2, d), BF16),
        ((2, 3, HALF // 2, d), BF16),
        ((4, RES, d), BF16),
        ((4, RES, d), BF16),
        ((3, RES, d), BF16),
        ((3, RES, d), BF16),
        ((16, 8, 128), F32),
        ((16, 8, 128), F32),
        ((lanes, 8, 128), F32),
        ((lanes, 8, 128), F32),
        ((8, STAT), F32),
        ((lanes, 8, 128), F32),
        ((16, d), BF16),
        ((seed_tokens.shape[1], 128), F32),
        ((TOK, TOK, d), BF16),
    ]
    return pl.pallas_call(
        kernel,
        out_shape=(
            jax.ShapeDtypeStruct((TOK, TOK, d), BF16),
            jax.ShapeDtypeStruct((1,), F32),
            jax.ShapeDtypeStruct((lanes, 128), F32),
            jax.ShapeDtypeStruct((2 * RES, d), BF16),
            jax.ShapeDtypeStruct((lanes, 128), F32),
        ),
        in_specs=[hbm, vmem, hbm, vmem, vmem, vmem, vmem],
        out_specs=(vmem, pl.BlockSpec(memory_space=pltpu.SMEM), vmem, vmem, vmem),
        scratch_shapes=[pltpu.VMEM(*s) for s in scratch]
        + [
            pltpu.SemaphoreType.DMA((COUNT,)),
            pltpu.SemaphoreType.DMA((COUNT,)),
            pltpu.SemaphoreType.DMA((4,)),
            pltpu.SemaphoreType.DMA((1,)),
        ],
        compiler_params=pltpu.CompilerParams(
            collective_id=0, has_side_effects=True, vmem_limit_bytes=60 * 2**20
        ),
        name="sae",
    )(residuals, slots, rows, dec, enc.reshape(lanes, 128), dead, seed_tokens)


def body(residuals, topk_slots, dictionary, enc_bias, dec_bias, dead_ids, seed_tokens):
    recon, unexplained, mass, new_rows, new_bias = fused(
        residuals, topk_slots, dictionary[0], dec_bias, enc_bias, dead_ids, seed_tokens
    )
    unexplained, recon, mass, new_rows, new_bias = handed_over(
        unexplained, recon, mass, new_rows, new_bias
    )
    return (recon, unexplained, mass.reshape(1, -1), new_rows[None], new_bias.reshape(1, -1))


def solution(mesh):
    split = Mesh(mesh.devices.reshape(4, 2, 4, 4), (Y, C, X, Z))
    placed = (
        P(None, LAYER_LAT, None),
        P(None, LAYER_LAT, None),
        P(LAYER, LAT, None),
        P(LAYER, LAT),
        P(LAYER, None),
        P(LAYER, None),
        P(LAYER, None),
    )
    return jax.shard_map(
        body,
        mesh=split,
        in_specs=placed,
        out_specs=(
            P(None, LAYER_LAT, None),
            P(LAYER),
            P(LAYER, LAT),
            P(LAYER, LAT, None),
            P(LAYER, LAT),
        ),
        check_vma=False,
    )
```

```python
import jax
import jax.numpy as jnp
from jax import lax
from jax.experimental import pallas as pl
from jax.experimental.pallas import tpu as pltpu
from jax.sharding import Mesh
from jax.sharding import PartitionSpec as P

Y, C, X, Z = "layer_0", "layer_1", "lat_0", "lat_1"
LAT = (X, Z)
LAYER = (Y, C)
LAYER_LAT = (Y, C, X, Z)
MESH = pl.DeviceIdType.MESH
NT = (((1,), (1,)), ((), ()))
F32 = jnp.float32
BF16 = jnp.bfloat16
TILE = 1024
STAT = 512
COLS = 2048
TOK = 8
HALF = 32
BLOCK = 256
RES = 8
GROUPS = TILE // 128

TO_LAYER, FIRST, AROUND, SQUARE, FAR, NEAR, SEEDS, LAST, LAST_SEEDS, FINAL, BACK, COUNT = (
    0, 8, 14, 24, 40, 42, 50, 56, 68, 74, 90, 98
)


def row_stats(w, decs, enc, inv, bias, norm, j):
    sq = None
    tile = pl.ds(j * STAT, STAT)
    for g in range(w.shape[1] // 128):
        piece = w[tile, g * 128 : (g + 1) * 128].astype(F32)
        a = piece * piece
        sq = a if sq is None else sq + a
    ones = jnp.ones((8, 128), F32)
    total = lax.dot_general(
        ones, sq, NT, precision=lax.Precision.HIGHEST, preferred_element_type=F32
    )
    parts = lax.dot_general(decs[...], w[tile, :], NT, preferred_element_type=F32)
    shift = jnp.sum(parts, axis=0, keepdims=True)
    n = jnp.sqrt(total + 1e-06)
    norm[...] += n
    iv = 1.0 / n
    for g in range(STAT // 128):
        at = slice(g * 128, (g + 1) * 128)
        row = j * (STAT // 128) + g
        inv[row] = iv[:, at]
        bias[row] = enc[pl.ds(row, 1), :] - shift[:, at] * iv[:, at]


def encode(feats, w, bits, inv, bias, mass, coef, p, between):
    tiles = w.shape[0] // TILE

    def product(j):
        p[j % 2] = lax.dot_general(
            feats[...], w[pl.ds(j * TILE, TILE), :], NT, preferred_element_type=F32
        )

    def activity(j):
        for g in range(GROUPS):
            row = j * GROUPS + g
            iv = inv[row]
            pre = p[j % 2, :, g * 128 : (g + 1) * 128].reshape(BLOCK // 8, 8, 128)
            count = ((bits[j] >> (4 * g)) & 15).astype(F32)
            total = jnp.maximum(pre * iv + bias[row], 0.0) * count
            mass[row] += jnp.sum(total, axis=0)
            coef[:, row * 128 : (row + 1) * 128] = (total * iv).reshape(BLOCK, 128).astype(BF16)

    product(0)
    for j in range(1, tiles):
        product(j)
        activity(j - 1)
        if j == 3:
            between()
    activity(tiles - 1)


def iota(shape, dim):
    return lax.broadcasted_iota(jnp.int32, shape, dim)


def seed_places(seeds, x, z):
    n = seeds[...]
    home, g, t = (n >> 3) & 15, n >> 7, n & 7
    xi, zi = home >> 2, home & 3
    is_a = g < 4
    far = jnp.where(is_a, zi - z, xi - x) & 3
    index = jnp.where(is_a, xi, zi)
    odd = (far & 1) == 1
    step = jnp.where(odd, 1 + ((g & 3) >> 1 << 1), far)
    inside = jnp.where(
        odd, (far >> 1) * 64 + index * 16 + (g & 1) * TOK, index * HALF + (g & 3) * TOK
    )
    place = step * BLOCK + jnp.where(is_a, 0, 128) + inside + t
    size = seeds.shape[1]
    row, col = iota((size, size), 0), iota((size, size), 1)
    k, h, i = row >> 6, (row >> 5) & 1, (row >> 3) & 3
    xr = jnp.where(h == 0, i, (x + k) & 3)
    zr = jnp.where(h == 0, (z + k) & 3, i)
    match = col == (xr * 4 + zr) * 16 + h * RES + (row & 7)
    ones = jnp.ones((size, 128), BF16)

    def column(v):
        kept = jnp.where(match, v.astype(F32), 0.0).astype(BF16)
        return jnp.dot(kept, ones, preferred_element_type=F32)

    return column(place >> 5) * 32.0 + column(place & 31)


def one_hot(places, count):
    spots = iota(places.shape, 1).astype(F32)
    return jnp.concatenate(
        [jnp.where(places - q * 128.0 == spots, 1.0, 0.0) for q in range(count // 128)], axis=1
    ).astype(BF16)


def kernel(
    res, slots, w_hbm, dec, enc, dead, seed_tokens,
    recon, unexplained, mass_out, new_rows, new_bias,
    w, aug, own, fa, fb, nf, bits, coef, p, part, fara, farb, near_in, picked, seeds, rsa, rsb,
    sa, sb, ta, tb, ssa, ssb, tsa, tsb, squares, finals, inv, bias, norm, mass, decs, places, rec,
    send, recv, wsem, osem,
):
    d = w.shape[1]
    lats = w.shape[0]
    y, c, x, z = (lax.axis_index(a) for a in (Y, C, X, Z))
    me = 2 * y + c
    here = 4 * x + z
    tokens = 4 * BLOCK

    def ring(at, step):
        return lax.rem(at + step, 4)

    def push(src, dst, n, device):
        return pltpu.make_async_remote_copy(
            src_ref=src, dst_ref=dst, send_sem=send.at[n], recv_sem=recv.at[n],
            device_id=device, device_id_type=MESH,
        )

    def local(src, dst, n):
        return pltpu.make_async_copy(src, dst, osem.at[n])

    sent = []

    def start(copies):
        for copy in copies:
            copy.start()
        sent.extend(copies)

    def arrive(copies):
        for copy in copies:
            copy.wait_recv()

    column = [(dy, dc) for dy in range(4) for dc in range(2) if dy or dc]
    plane = [(dx, dz) for dx in range(4) for dz in range(4) if dx or dz]

    def in_column(dy, dc):
        return {Y: ring(y, dy), C: lax.rem(c + dc, 2)}

    def in_plane(dx, dz):
        return {X: ring(x, dx), Z: ring(z, dz)}

    barrier = pltpu.get_barrier_semaphore()
    for dy, dc in column:
        pl.semaphore_signal(barrier, inc=1, device_id=in_column(dy, dc), device_id_type=MESH)
    for dx, dz in plane:
        pl.semaphore_signal(barrier, inc=1, device_id=in_plane(dx, dz), device_id_type=MESH)

    fill = local(res, aug.at[:, :, pl.ds(0, d)], 0)
    fill.start()
    rows = lats // 4
    loads = [
        pltpu.make_async_copy(w_hbm.at[pl.ds(q * rows, rows)], w.at[pl.ds(q * rows, rows)], wsem.at[q])
        for q in range(4)
    ]
    ids = slots[...]
    place = jnp.where(ids >= 0, ids - (iota(ids.shape, 2) >> 2) * lats, lats)
    tail = jnp.concatenate([(place >> 6).astype(F32), (place & 63).astype(F32)], axis=2)
    aug[:, :, pl.ds(d, 128)] = tail.astype(BF16)
    fill.wait()
    pl.semaphore_wait(barrier, len(column) + len(plane))

    to_layer = []
    for dy, dc in column:
        g = 2 * ring(y, dy) + lax.rem(c + dc, 2)
        to_layer.append(push(aug.at[g], own.at[me], TO_LAYER + 2 * dy + dc, in_column(dy, dc)))
    start(to_layer)
    for load in loads:
        load.start()
    own[me] = aug[me]

    high = dec[...].astype(BF16).astype(F32)
    middle = (dec[...] - high).astype(BF16).astype(F32)
    low = dec[...] - high - middle
    which = iota((16, d), 0)
    decs[...] = jnp.where(
        which == 0, high, jnp.where(which == 1, middle, jnp.where(which == 2, low, 0.0))
    ).astype(BF16)
    norm[...] = jnp.zeros_like(norm)
    mass[...] = jnp.zeros_like(mass)

    def stats(q):
        loads[q].wait()
        per = rows // STAT
        lax.fori_loop(
            q * per, (q + 1) * per, lambda j, _: row_stats(w, decs, enc, inv, bias, norm, j), None
        )

    stats(0)
    arrive(to_layer)

    half = TOK // 2
    first = []
    for k in (1, 3, 2):
        first.append(push(own.at[pl.ds(0, half)], fa.at[z, x], FIRST + k - 1, {X: ring(x, k)}))
        first.append(push(own.at[pl.ds(half, half)], fb.at[x, z], FIRST + 2 + k, {Z: ring(z, k)}))
    start(first)
    fa[z, x] = own[pl.ds(0, half)]
    fb[x, z] = own[pl.ds(half, half)]

    def add_squares(g, acc):
        v = own[g, :, pl.ds(0, d)].astype(F32)
        return acc + v * v

    square = jnp.sum(lax.fori_loop(0, TOK, add_squares, jnp.zeros((TOK, d), F32)))
    squares[here] = jnp.full((8, 128), square, F32)
    square_copies = [
        push(squares.at[here], squares.at[here], SQUARE + 4 * dx + dz, in_plane(dx, dz))
        for dx, dz in plane
    ]
    start(square_copies)
    for q in (1, 2, 3):
        stats(q)
    places[...] = seed_places(seed_tokens, x, z)
    arrive(first)

    def beside(h):
        rows = pl.ds(2 * h, 2)
        out = []
        for e, k in enumerate((1, 3)):
            n = AROUND + 2 + 4 * h + 2 * e
            out.append(push(fa.at[z, :, rows], fa.at[z, :, rows], n, {Z: ring(z, k)}))
            out.append(push(fb.at[x, :, rows], fb.at[x, :, rows], n + 1, {X: ring(x, k)}))
        return out

    across = [
        push(fa.at[z], fa.at[z], AROUND, {Z: ring(z, 2)}),
        push(fb.at[x], fb.at[x], AROUND + 1, {X: ring(x, 2)}),
    ]
    beside_a, beside_b = beside(0), beside(1)
    start(beside_a)
    sent.extend(across + beside_b)
    arrive(square_copies)
    scale = lax.rsqrt(jnp.sum(squares[...], axis=0)[0:1, 0:1] / (tokens * d))

    pick_row = iota((128, 512), 0)
    pick_slot = (iota((128, 512), 1) >> 7) + 4 * here
    pick = jnp.where(pick_row == pick_slot, 64.0, 0.0) + jnp.where(pick_row == pick_slot + 64, 1.0, 0.0)
    pick = pick.astype(BF16)

    def near_share(h):
        devices = ({Z: ring(z, 1)}, {Z: ring(z, 3)}, {X: ring(x, 1)}, {X: ring(x, 3)})
        return [
            push(part.at[1 + 2 * h, pl.ds(e * 64, 64)], near_in.at[h, e], NEAR + 4 * h + e, device)
            for e, device in enumerate(devices)
        ]

    near_a, near_b = near_share(0), near_share(1)
    far = [
        push(part.at[2, pl.ds(0, 128)], fara, FAR, {Z: ring(z, 2)}),
        push(part.at[2, pl.ds(128, 128)], farb, FAR + 1, {X: ring(x, 2)}),
    ]
    sent.extend(far + near_a + near_b)

    def decode(step, source):
        @pl.loop(0, d // COLS)
        def _(n):
            at = pl.ds(pl.multiple_of(n * COLS, COLS), COLS)
            v = jnp.dot(source[...], w[:, at], preferred_element_type=F32)
            part[step, :, at] = v.astype(BF16)

    def block(step, _):
        close = step % 2

        @pl.when(step == 1)
        def _():
            arrive(beside_a)

        @pl.when(step == 2)
        def _():
            arrive(across)

        @pl.when(step == 3)
        def _():
            arrive(beside_b)

        lane = iota((16, 8, 128), 2)
        for h, buf, at in ((0, fa, z), (1, fb, x)):

            def chunk(m, cols):
                away = (1 - close) * step + close * (1 + m // 4 * 2)
                index = (1 - close) * (m // 2) + close * (m % 4)
                low = (1 - close) * (m % 2 * 2) + close * (step - 1)
                v = buf[ring(at, away), index, pl.ds(low, 2), :, cols]
                return v.astype(F32).reshape(16, cols.size)

            def normalize(m, _, h=h, chunk=chunk):
                v = chunk(m, pl.ds(0, d)) * scale
                nf[step, pl.ds(h * 128 + m * 16, 16), :] = v.astype(BF16)

            lax.fori_loop(0, 8, normalize, None)
            tails = [chunk(m, pl.ds(d, 128)) for m in range(8)]
            tails = jnp.concatenate(tails, axis=0).astype(BF16)
            found = jnp.dot(tails, pick, preferred_element_type=F32).astype(jnp.int32)
            fields = [jnp.zeros((16, 8, 128), jnp.int32) for _ in range(lats // TILE)]
            for s in range(4):
                v = found[:, s * 128 : (s + 1) * 128].reshape(16, 8, 128)
                one = jnp.where((v & 127) == lane, jnp.int32(1) << (((v >> 7) & 7) << 2), 0)
                fields = [f + jnp.where(v >> 10 == j, one, 0) for j, f in enumerate(fields)]
            for j, f in enumerate(fields):
                bits[j, pl.ds(16 * h, 16)] = f

        def between():
            @pl.when(step == 0)
            def _():
                for copy in across:
                    copy.start()

        mine = jnp.minimum(step, 1)
        encode(nf.at[step], w, bits, inv, bias, mass, coef.at[mine], p, between)

        @pl.when(step > 0)
        def _():
            decode(step, coef.at[1])

        @pl.when(step == 1)
        def _():
            for copy in beside_b + near_a:
                copy.start()

        @pl.when(step == 2)
        def _():
            for copy in far:
                copy.start()

        @pl.when(step == 3)
        def _():
            for copy in near_b:
                copy.start()

    lax.fori_loop(0, 4, block, None)

    hot = one_hot(places[...], tokens)

    @pl.loop(0, d // 1024)
    def _(n):
        at = pl.ds(pl.multiple_of(n * 1024, 1024), 1024)
        others = part[1:, :, at].reshape(3 * BLOCK, 1024)
        picked[:, at] = jnp.dot(hot[:, BLOCK:], others, preferred_element_type=F32)

    decode(0, coef.at[0])

    def combine(h):
        for i in range(4):
            at, in_h = pl.ds(i * HALF + h * 16, 16), pl.ds(i * 16, 16)
            for to, got, lo, e in ((sa, fara, 0, 0), (sb, farb, 128, 2)):
                v = part[0, pl.ds(lo + i * HALF + h * 16, 16), :].astype(F32) + got[at, :].astype(F32)
                v = v + near_in[h, e, in_h, :].astype(F32) + near_in[h, e + 1, in_h, :].astype(F32)
                to[h, i] = v.astype(BF16)
        copies = []
        for k in (2, 1, 3):
            n = LAST + 6 * h + k - 1
            copies.append(push(sa.at[h, ring(x, k)], ta.at[h, k - 1], n, {X: ring(x, k)}))
            copies.append(push(sb.at[h, ring(z, k)], tb.at[h, k - 1], n + 3, {Z: ring(z, k)}))
        start(copies)
        return copies

    arrive(far)
    arrive(near_a)
    last = [combine(0)]

    @pl.loop(0, d // 1024)
    def _(n):
        at = pl.ds(pl.multiple_of(n * 1024, 1024), 1024)
        v = jnp.dot(hot[:, :BLOCK], part[0, :, at], preferred_element_type=F32) + picked[:, at]
        seeds[:, :, :, :, at] = v.reshape(4, 2, 4, RES, 1024).astype(BF16)

    seed_copies = []
    for k in (2, 1, 3):
        seed_copies.append(push(seeds.at[k, 0], rsa.at[k - 1], SEEDS + k - 1, {Z: ring(z, k)}))
        seed_copies.append(push(seeds.at[k, 1], rsb.at[k - 1], SEEDS + 2 + k, {X: ring(x, k)}))
    arrive(near_b)
    last.append(combine(1))
    start(seed_copies)

    def add_tokens(q, acc):
        for k in range(4):
            acc = acc + nf[k, pl.ds(q * 16, 16), :].astype(F32)
        return acc

    sums = lax.fori_loop(0, BLOCK // 16, add_tokens, jnp.zeros((16, d), F32))
    means = jnp.sum(sums, axis=0, keepdims=True) / tokens
    my_places = jnp.concatenate(
        [places[pl.ds(x * RES, RES), :], places[pl.ds(4 * RES + z * RES, RES), :]], axis=0
    )
    seed_feats = jnp.dot(
        one_hot(my_places, tokens), nf[...].reshape(tokens, d), preferred_element_type=F32
    )
    norm_sum = jnp.sum(norm[...]) / 8.0

    def back(g):
        device = {Y: g // 2 + 0 * y, C: g % 2 + 0 * c}
        return pltpu.make_async_remote_copy(
            src_ref=rec.at[g], dst_ref=recon.at[me], send_sem=send.at[BACK + g],
            recv_sem=recv.at[BACK + me], device_id=device, device_id_type=MESH,
        )

    def elsewhere(g, act):
        @pl.when(me != g)
        def _():
            act()

    numerator = denominator = 0.0
    for h in range(2):
        arrive(last[h])
        for mine_sum, got, g, lo in (
            (sa.at[h, x], ta, 2 * h, x * HALF),
            (sb.at[h, z], tb, half + 2 * h, 128 + z * HALF),
        ):
            v = mine_sum[...].astype(F32)
            for k in range(3):
                v = v + got[h, k].astype(F32)
            v = v + dec[...]
            rec[pl.ds(g, 2)] = v.reshape(2, TOK, d).astype(BF16)
            for e in (g, g + 1):
                elsewhere(e, lambda e=e: back(e).start())
            feats = nf[0, pl.ds(lo + 16 * h, 16), :].astype(F32)
            e, m = feats - v, feats - means
            numerator = numerator + jnp.sum(e * e)
            denominator = denominator + jnp.sum(m * m)
    recon[me] = rec[me]
    kind = iota((8, 128), 0)
    finals[here] = jnp.where(kind == 0, numerator, jnp.where(kind == 1, denominator, norm_sum))
    final_copies = [
        push(finals.at[here], finals.at[here], FINAL + 4 * dx + dz, in_plane(dx, dz)) for dx, dz in plane
    ]
    start(final_copies)
    arrive(seed_copies)

    def add_seeds(q, _):
        for to, got, h in ((ssa, rsa, 0), (ssb, rsb, 1)):
            v = seeds[0, h, q].astype(F32)
            for k in range(3):
                v = v + got[k, q].astype(F32)
            to[q] = v.astype(BF16)

    lax.fori_loop(0, 4, add_seeds, None)
    last_seeds = []
    for k in (1, 3, 2):
        last_seeds.append(push(ssa.at[ring(x, k)], tsa.at[k - 1], LAST_SEEDS + k - 1, {X: ring(x, k)}))
        last_seeds.append(push(ssb.at[ring(z, k)], tsb.at[k - 1], LAST_SEEDS + 2 + k, {Z: ring(z, k)}))
    start(last_seeds)

    lanes = lats // 128
    gone = dead[...] - here * lats
    at_row = jnp.where(iota((lanes, gone.shape[1]), 0) == gone >> 7, 1.0, 0.0).astype(BF16)
    at_lane = jnp.where(iota((128, gone.shape[1]), 0) == (gone & 127), 1.0, 0.0).astype(BF16)
    hits = lax.dot_general(at_row, at_lane, NT, preferred_element_type=F32)
    new_bias[...] = jnp.where(hits > 0.5, 0.0, enc[...])
    mass_out[...] = jnp.sum(mass[...], axis=1)

    arrive(last_seeds)
    estimates = []
    for mine_sum, got in ((ssa.at[x], tsa), (ssb.at[z], tsb)):
        v = mine_sum[...].astype(F32)
        for k in range(3):
            v = v + got[k].astype(F32)
        estimates.append(v + dec[...])
    errors = seed_feats - jnp.concatenate(estimates, axis=0)
    seed_norm = jnp.sqrt(jnp.sum(errors * errors, axis=1, keepdims=True) + 1e-06)
    unit = errors / seed_norm
    arrive(final_copies)
    total = jnp.sum(finals[...], axis=0)
    ratio = total[0:1, :] / total[1:2, :]
    unexplained[0] = ratio[0, 0]
    new_rows[...] = (unit * (total[2:3, 0:1] / (lats * 16))).astype(BF16)
    for g in range(TOK):
        def settle(g=g):
            pltpu.make_async_remote_copy(
                src_ref=rec.at[g], dst_ref=recon.at[g], send_sem=send.at[BACK + g],
                recv_sem=recv.at[BACK + g], device_id={Y: ring(y, 1)}, device_id_type=MESH,
            ).wait()

        elsewhere(g, settle)
    for copy in sent:
        copy.wait_send()


def hand_over(*refs):
    count = len(refs) // 2
    refs[count][0] = refs[0][0]
    for i in range(1, count):
        refs[count + i][...] = refs[i][...]


def handed_over(*arrays):
    specs = [pl.BlockSpec(memory_space=pltpu.SMEM)]
    specs += [pl.BlockSpec(memory_space=pltpu.VMEM)] * (len(arrays) - 1)
    return pl.pallas_call(
        hand_over,
        out_shape=tuple(jax.ShapeDtypeStruct(a.shape, a.dtype) for a in arrays),
        in_specs=specs,
        out_specs=tuple(specs),
        name="hand_over",
    )(*arrays)


def fused(residuals, slots, rows, dec, enc, dead, seed_tokens):
    lats, d = rows.shape
    wide = d + 128
    lanes = lats // 128
    vmem = pl.BlockSpec(memory_space=pltpu.VMEM)
    hbm = pl.BlockSpec(memory_space=pl.ANY)
    half = TOK // 2
    scratch = [
        ((lats, d), BF16),
        ((TOK, TOK, wide), BF16),
        ((TOK, TOK, wide), BF16),
        ((4, 4, half, TOK, wide), BF16),
        ((4, 4, half, TOK, wide), BF16),
        ((4, BLOCK, d), BF16),
        ((lats // TILE, BLOCK // 8, 8, 128), jnp.int32),
        ((2, BLOCK, lats), BF16),
        ((2, BLOCK, TILE), F32),
        ((4, BLOCK, d), BF16),
        ((128, d), BF16),
        ((128, d), BF16),
        ((2, 4, 64, d), BF16),
        ((seed_tokens.shape[1], d), F32),
        ((4, 2, 4, RES, d), BF16),
        ((3, 4, RES, d), BF16),
        ((3, 4, RES, d), BF16),
        ((2, 4, HALF // 2, d), BF16),
        ((2, 4, HALF // 2, d), BF16),
        ((2, 3, HALF // 2, d), BF16),
        ((2, 3, HALF // 2, d), BF16),
        ((4, RES, d), BF16),
        ((4, RES, d), BF16),
        ((3, RES, d), BF16),
        ((3, RES, d), BF16),
        ((16, 8, 128), F32),
        ((16, 8, 128), F32),
        ((lanes, 8, 128), F32),
        ((lanes, 8, 128), F32),
        ((8, STAT), F32),
        ((lanes, 8, 128), F32),
        ((16, d), BF16),
        ((seed_tokens.shape[1], 128), F32),
        ((TOK, TOK, d), BF16),
    ]
    return pl.pallas_call(
        kernel,
        out_shape=(
            jax.ShapeDtypeStruct((TOK, TOK, d), BF16),
            jax.ShapeDtypeStruct((1,), F32),
            jax.ShapeDtypeStruct((lanes, 128), F32),
            jax.ShapeDtypeStruct((2 * RES, d), BF16),
            jax.ShapeDtypeStruct((lanes, 128), F32),
        ),
        in_specs=[hbm, vmem, hbm, vmem, vmem, vmem, vmem],
        out_specs=(vmem, pl.BlockSpec(memory_space=pltpu.SMEM), vmem, vmem, vmem),
        scratch_shapes=[pltpu.VMEM(*s) for s in scratch]
        + [
            pltpu.SemaphoreType.DMA((COUNT,)),
            pltpu.SemaphoreType.DMA((COUNT,)),
            pltpu.SemaphoreType.DMA((4,)),
            pltpu.SemaphoreType.DMA((1,)),
        ],
        compiler_params=pltpu.CompilerParams(
            collective_id=0, has_side_effects=True, vmem_limit_bytes=60 * 2**20
        ),
        name="sae",
    )(residuals, slots, rows, dec, enc.reshape(lanes, 128), dead, seed_tokens)


def body(residuals, topk_slots, dictionary, enc_bias, dec_bias, dead_ids, seed_tokens):
    recon, unexplained, mass, new_rows, new_bias = fused(
        residuals, topk_slots, dictionary[0], dec_bias, enc_bias, dead_ids, seed_tokens
    )
    unexplained, recon, mass, new_rows, new_bias = handed_over(
        unexplained, recon, mass, new_rows, new_bias
    )
    return (recon, unexplained, mass.reshape(1, -1), new_rows[None], new_bias.reshape(1, -1))


def solution(mesh):
    split = Mesh(mesh.devices.reshape(4, 2, 4, 4), (Y, C, X, Z))
    placed = (
        P(None, LAYER_LAT, None),
        P(None, LAYER_LAT, None),
        P(LAYER, LAT, None),
        P(LAYER, LAT),
        P(LAYER, None),
        P(LAYER, None),
        P(LAYER, None),
    )
    return jax.shard_map(
        body,
        mesh=split,
        in_specs=placed,
        out_specs=(
            P(None, LAYER_LAT, None),
            P(LAYER),
            P(LAYER, LAT),
            P(LAYER, LAT, None),
            P(LAYER, LAT),
        ),
        check_vma=False,
    )
```
